512 devices in a mesh: mesh: 32 (over x_hi, z, core), band: 16 (over x_lo, y).
Axes of the slice: x: 4 (x_hi: 2, x_lo: 2; x = x_hi * 2 + x_lo), y: 8, z: 8, core: 2. Of those that a mesh axis runs over, the one named last changes fastest.
Arguments:
- filter_block: bfloat16 [512, 196608], P('band', 'mesh'), may hold values from -6 to 6
- local_pot: float32 [196608], P('mesh'), may hold values from 0.5 to 2
- cell_scale: float32 [4096], P('mesh'), may hold values from 0.5 to 2
- cell_kernel: bfloat16 [125, 125], replicated
- cell_map: int32 [125, 4096], P(None, 'mesh'), may hold values from 0 to 8191, as said below
- neighbour_ids: int32 [32, 14], P('mesh'), may hold values from 0 to 31, as said below
- send_nodes: int32 [32, 14, 64], P('mesh'), may hold values from 0 to 6143
- rotation_rows: bfloat16 [512, 512], P('band'), may hold values from -0.25 to 0.25
- panel_owner: int32 [2], replicated, may hold values from 0 to 15
Outputs:
- filtered: bfloat16 [512, 196608], P('band', 'mesh')
- rotated: bfloat16 [512, 196608], P(None, ('mesh', 'band'))
- state_energy: float32 [512], P('band')
The draws below stay inside these ranges and needn't reach their ends.
Inputs may be any that keep to these rules, and one draw needn't show every extreme that they name: `neighbour_ids`: row p lists 14 distinct partitions other than p; q is listed in row p exactly when p is listed in row q. `cell_map`: in the columns of partition p's cells an entry below 6144 names an owned node of p, and an entry 6144 + q*64 + g names slot g of a partition q listed in row p of neighbour_ids.
All inputs are finite; a program needn't handle non-finite values.
Results may differ from the reference program's by a relative error of at most 0.0059.
Values may be sent and summed in bfloat16 or wider, within the bound.
No kernel may reach another device: no remote copies, remote signals or barrier semaphores. Data moves between devices by JAX's collectives and lax.ppermute only.
A program may use at most 64 MiB of HBM per device.

```python
import math
import jax
import jax.numpy as jnp
from jax import lax

STATES = 512
NPE = 125
GHOST = 64
PSTEPS = 2
CELLS_DEV = 128
STATE_DEV = 32
NBR = 14
NODE_DEV = 6144
EXT = 8192
NODES = 196608
CELLS = 4096
N_MESH = 32
N_BAND = 16


def neighbour_table(key):
    ordering = jax.random.permutation(jax.random.fold_in(key, 11), N_MESH).astype(jnp.int32)
    position = jnp.zeros((N_MESH,), jnp.int32).at[ordering].set(jnp.arange(N_MESH, dtype=jnp.int32))
    half_count = NBR // 2
    offsets = jnp.concatenate([jnp.arange(1, half_count + 1), -jnp.arange(1, half_count + 1)]).astype(jnp.int32)
    return ordering[(position[:, None] + offsets[None, :]) % N_MESH]


def draw_neighbour_ids(key, part):
    return neighbour_table(key)


def draw_cell_map(key, part):
    neighbours = neighbour_table(key)
    entry_count = NPE * CELLS_DEV
    covered = NBR * GHOST

    def one_part(part_id):
        part_key = jax.random.fold_in(jax.random.fold_in(key, 23), part_id)
        keys = jax.random.split(part_key, 5)
        entries = jnp.arange(entry_count, dtype=jnp.int32)
        own_random = jax.random.randint(keys[0], (entry_count,), 0, NODE_DEV, dtype=jnp.int32)
        is_ghost = jax.random.randint(keys[1], (entry_count,), 0, 3, dtype=jnp.int32) == 0
        chosen = jax.random.randint(keys[2], (entry_count,), 0, NBR, dtype=jnp.int32)
        slots = jax.random.randint(keys[3], (entry_count,), 0, GHOST, dtype=jnp.int32)
        row_list = neighbours[part_id]
        ghost_random = NODE_DEV + row_list[chosen] * GHOST + slots
        values_out = jnp.where(is_ghost, ghost_random, own_random)
        fixed_ghost = NODE_DEV + row_list[entries // GHOST % NBR] * GHOST + entries % GHOST
        fixed_own = (entries - covered) % NODE_DEV
        values_out = jnp.where(entries < covered, fixed_ghost, jnp.where(entries < covered + NODE_DEV, fixed_own, values_out))
        shuffle = jax.random.permutation(keys[4], entry_count)
        values_out = values_out[shuffle]
        return values_out.reshape(CELLS_DEV, NPE).T
    all_maps = lax.map(one_part, jnp.arange(N_MESH, dtype=jnp.int32))
    return all_maps.transpose(1, 0, 2).reshape(NPE, N_MESH * CELLS_DEV).astype(jnp.int32)


def draw_cell_kernel(key, part):
    keys = jax.random.split(key, 2)
    off_part = jax.random.normal(keys[0], (NPE, NPE), jnp.float32)
    off_part = off_part * (0.6 / jnp.sqrt(jnp.float32(NPE)))
    diagonal = jax.random.uniform(keys[1], (NPE,), jnp.float32, 1.5, 3.0)
    identity = jnp.eye(NPE, dtype=jnp.float32)
    return (off_part * (1.0 - identity) + identity * diagonal[:, None]).astype(jnp.bfloat16)


def with_ends(values, stream_key, smallest, high):
    index_at = [jax.random.randint(jax.random.fold_in(stream_key, axis), (), 0, length) for axis, length in enumerate(values.shape)]
    longest = values.shape.index(max(values.shape))
    next_to = index_at[:longest] + [(index_at[longest] + 1) % values.shape[longest]] + index_at[longest + 1:]
    return values.at[tuple(index_at)].set(smallest).at[tuple(next_to)].set(high)


def block_levels(key, dims, shards, least, top_value):
    def one(dim, shards_of):
        draws = jax.random.uniform(jax.random.fold_in(jax.random.fold_in(key, 6), dim), (shards_of,), jnp.float32, least / len(shards), top_value / len(shards))
        return jnp.repeat(jnp.exp(draws), dims[dim] // shards_of).reshape((-1,) + (1,) * (len(dims) - dim - 1))

    gain = one(*shards[0])
    for cut in shards[1:]:
        gain = gain * one(*cut)
    return gain


def bell_draw(stream_key, dims, width, most, shards=(), kind=jnp.bfloat16):
    values = jax.random.normal(stream_key, dims, jnp.float32) * width
    if len(shards) > 0:
        values = block_levels(stream_key, dims, shards, -0.22, 0.18) * values
    return jnp.clip(values, min=-most, max=most).astype(kind)


def setup_inputs(seed: int = 0) -> dict:
    key_of = jax.random.split(jax.random.key(seed), 10)
    return {
        "filter_block": bell_draw(key_of[0], (STATES, NODES), 1.0, 6.0, ((0, 16), (1, 32))),
        "local_pot": jnp.clip(0.5 + 1.5 * jax.random.uniform(key_of[1], (NODES,), jnp.float32) ** block_levels(key_of[1], (NODES,), ((0, 32),), -0.2, 0.2), 0.5, 2.0),
        "cell_scale": jnp.clip(jnp.exp(math.log(2.0) - 1.3862944 * jax.random.uniform(key_of[2], (CELLS,), jnp.float32) ** block_levels(key_of[2], (CELLS,), ((0, 32),), -0.2, 0.2)), 0.5, 2.0),
        "cell_kernel": draw_cell_kernel(jax.random.fold_in(key_of[9], 71), 0),
        "cell_map": draw_cell_map(jax.random.fold_in(key_of[9], 71), 0),
        "neighbour_ids": draw_neighbour_ids(jax.random.fold_in(key_of[9], 71), 0),
        "send_nodes": with_ends(jax.random.randint(key_of[6], (N_MESH, NBR, GHOST), 0, NODE_DEV), jax.random.fold_in(key_of[6], 1), 0, NODE_DEV - 1).astype(jnp.int32),
        "rotation_rows": bell_draw(key_of[7], (STATES, STATES), STATES ** -0.5, 0.25, ((0, 16),)),
        "panel_owner": jax.random.randint(key_of[8], (PSTEPS,), 0, N_BAND).astype(jnp.int32),
    }


center = 6.0
half_width = 4.0


def ghost_block(state_field, neighbour_ids, send_nodes, part_id):
    matches = neighbour_ids == part_id
    row_index = jnp.sum(jnp.where(matches[:, :, None], send_nodes, 0), axis=1).astype(jnp.int32)
    present = jnp.any(matches, axis=1)
    owners = jnp.arange(N_MESH, dtype=jnp.int32)[:, None]
    picked = state_field[:, owners, row_index]
    picked = jnp.where(present[None, :, None], picked, jnp.zeros_like(picked))
    return picked.reshape(STATES, N_MESH * GHOST)


def reference(filter_block, local_pot, cell_scale, cell_kernel, cell_map, neighbour_ids, send_nodes, rotation_rows, panel_owner):
    field_zero = filter_block.reshape(STATES, N_MESH, NODE_DEV)
    potential = local_pot.reshape(N_MESH, NODE_DEV)
    scales = cell_scale.reshape(N_MESH, CELLS_DEV)
    all_maps = cell_map.reshape(NPE, N_MESH, CELLS_DEV)
    kernel = cell_kernel.astype(jnp.float32)

    def operate(state_field, part_id):
        own_rows = state_field[:, part_id]
        ghosts = ghost_block(state_field, neighbour_ids, send_nodes, part_id)
        extended = jnp.concatenate([own_rows, ghosts], axis=1)
        cell_nodes = all_maps[:, part_id]
        gathered = jnp.take(extended, cell_nodes, axis=1).astype(jnp.float32)
        product = jnp.einsum("ab,sbc->sac", kernel, gathered) * scales[part_id]
        totals = jnp.zeros((STATES, EXT), jnp.float32).at[:, cell_nodes.reshape(-1)].add(product.reshape(STATES, -1))
        return totals[:, :NODE_DEV] + potential[part_id] * own_rows.astype(jnp.float32), own_rows

    def first_step(part_id):
        image_zero, own_rows = operate(field_zero, part_id)
        return ((image_zero - center * own_rows.astype(jnp.float32)) / half_width).astype(jnp.bfloat16)

    field_one = lax.map(first_step, jnp.arange(N_MESH, dtype=jnp.int32)).transpose(1, 0, 2)

    def second(part_id):
        image_one, own_rows = operate(field_one, part_id)
        own_float = own_rows.astype(jnp.float32)
        energy = jnp.sum(own_float * image_one, axis=1)
        start_field = field_zero[:, part_id].astype(jnp.float32)
        next_field = (2.0 * (image_one - center * own_float) / half_width - start_field).astype(jnp.bfloat16)
        return next_field, energy

    field_two, energies = lax.map(second, jnp.arange(N_MESH, dtype=jnp.int32))
    state_energy = jnp.sum(energies, axis=0) / NODES
    filtered = field_two.transpose(1, 0, 2).reshape(STATES, NODES)
    totals = jnp.zeros((STATES, NODES), jnp.float32)
    for step_id in range(PSTEPS):
        first_row = (panel_owner[step_id] * STATE_DEV).astype(jnp.int32)
        picked = lax.dynamic_slice_in_dim(filtered, first_row, STATE_DEV, 0).astype(jnp.float32)
        coefficients = lax.dynamic_slice_in_dim(rotation_rows, first_row, STATE_DEV, 0).astype(jnp.float32)
        totals = totals + jnp.dot(coefficients.T, picked, preferred_element_type=jnp.float32)
    return filtered, totals.astype(jnp.bfloat16), state_energy
```

```python
import functools

import jax
import jax.numpy as jnp
from jax import lax
from jax.experimental import pallas as pl
from jax.experimental.pallas import tpu as pltpu
from jax.sharding import PartitionSpec as P

center = 6.0
half_width = 4.0
LO = 512
GLO = 128
STEP = 8


def onehot(rows, width):
    level = lax.broadcasted_iota(jnp.int32, (width, 128), 0)
    parts = [jnp.where(level == row, 1.0, 0.0).astype(jnp.bfloat16) for row in rows]
    return jnp.concatenate(parts, axis=1)


def pick(table, indices, count, width):
    shift = width.bit_length() - 1
    rows = [indices[k : k + 1, :] for k in range(indices.shape[0])]
    low = [jnp.bitwise_and(row, width - 1) for row in rows]
    high = [jnp.right_shift(row, shift) for row in rows]
    product = jnp.dot(table, onehot(low, width), preferred_element_type=jnp.float32)
    groups = table.shape[0] // count
    picked = []
    for k in range(len(rows)):
        total = jnp.zeros((count, 128), jnp.float32)
        for group in range(groups):
            part = product[group * count : (group + 1) * count, k * 128 : (k + 1) * 128]
            total = jnp.where(high[k] == group, part, total)
        picked.append(total)
    return picked


def stack_groups(field_ref, table_ref, count, width):
    for group in range(field_ref.shape[1] // width):
        table_ref[group * count : (group + 1) * count, :] = field_ref[
            :, group * width : (group + 1) * width
        ]


def pack_sends(table_ref, send_ref, nbr_ref, out_ref, count):
    out_ref[...] = jnp.zeros(out_ref.shape, out_ref.dtype)
    picked = pick(table_ref[...], send_ref[...], count, LO)
    half = count // 2
    for k, part in enumerate(picked):
        for side in range(2):
            block = part[:, side * 64 : (side + 1) * 64]
            tile = jnp.concatenate([block[:half], block[half:]], axis=1)
            out_ref[nbr_ref[2 * k + side]] = tile.astype(jnp.bfloat16)


def pack_kernel(nbr_ref, field_ref, send_ref, out_ref, table_ref):
    count = field_ref.shape[0]
    stack_groups(field_ref, table_ref, count, LO)
    pack_sends(table_ref, send_ref, nbr_ref, out_ref, count)


def own_kernel(field_ref, index_ref, out_ref, table_ref):
    count = field_ref.shape[0]
    stack_groups(field_ref, table_ref, count, LO)

    def body(step, carry):
        base = pl.multiple_of(step * STEP, STEP)
        picked = pick(table_ref[...], index_ref[pl.ds(base, STEP), :], count, LO)
        for k in range(STEP):
            out_ref[base + k] = picked[k].astype(jnp.bfloat16)
        return carry

    lax.fori_loop(0, index_ref.shape[0] // STEP, body, 0)


def apply_body(
    nbr_ref, field_ref, own_ref, recv_ref, index_ref, ghost_index_ref, kernel_ref,
    scale_ref, ghost_ref, nodes_ref, product_ref, total_ref,
):
    count = field_ref.shape[0]
    half = count // 2
    steps = index_ref.shape[0] // STEP
    for k in range(ghost_ref.shape[0] // count):
        left = recv_ref[nbr_ref[2 * k]]
        right = recv_ref[nbr_ref[2 * k + 1]]
        ghost_ref[k * count : k * count + half, :] = jnp.concatenate(
            [left[:, :64], right[:, :64]], axis=1
        )
        ghost_ref[k * count + half : (k + 1) * count, :] = jnp.concatenate(
            [left[:, 64:], right[:, 64:]], axis=1
        )

    def ghosts(step, carry):
        base = pl.multiple_of(step * STEP, STEP)
        picked = pick(ghost_ref[...], ghost_index_ref[pl.ds(base, STEP), :], count, GLO)
        for k in range(STEP):
            nodes_ref[base + k] = picked[k] + own_ref[base + k].astype(jnp.float32)
        return carry

    lax.fori_loop(0, steps, ghosts, 0)

    for state in range(count):
        columns = nodes_ref[:, state, :].astype(jnp.bfloat16)
        product = jnp.dot(kernel_ref[...], columns, preferred_element_type=jnp.float32)
        product_ref[:, state, :] = product * scale_ref[...]

    total_ref[...] = jnp.zeros(total_ref.shape, jnp.float32)
    groups = total_ref.shape[0] // count
    zero = jnp.zeros((count, 128), jnp.bfloat16)

    def scatter(step, carry):
        base = pl.multiple_of(step * STEP, STEP)
        indices = index_ref[pl.ds(base, STEP), :]
        rows = [indices[k : k + 1, :] for k in range(STEP)]
        low = [jnp.bitwise_and(row, LO - 1) for row in rows]
        high = [jnp.right_shift(row, LO.bit_length() - 1) for row in rows]
        parts = []
        for k in range(STEP):
            value = product_ref[base + k].astype(jnp.float32)
            parts.append(
                jnp.concatenate(
                    [
                        jnp.where(high[k] == group, value, 0.0).astype(jnp.bfloat16)
                        for group in range(groups)
                    ],
                    axis=0,
                )
            )
        left = jnp.concatenate(parts, axis=1)
        total_ref[...] += lax.dot_general(
            left, onehot(low, LO), (((1,), (1,)), ((), ())), preferred_element_type=jnp.float32
        )
        return carry

    lax.fori_loop(0, steps, scatter, 0)


def first_kernel(
    nbr_ref, field_ref, own_ref, recv_ref, index_ref, ghost_index_ref, kernel_ref, scale_ref,
    pot_ref, send_ref, next_ref, out_ref, table_ref, ghost_ref, nodes_ref, product_ref, total_ref,
):
    apply_body(
        nbr_ref, field_ref, own_ref, recv_ref, index_ref, ghost_index_ref, kernel_ref,
        scale_ref, ghost_ref, nodes_ref, product_ref, total_ref,
    )
    count = field_ref.shape[0]
    for group in range(field_ref.shape[1] // LO):
        lanes = slice(group * LO, (group + 1) * LO)
        rows = slice(group * count, (group + 1) * count)
        start = field_ref[:, lanes].astype(jnp.float32)
        image = total_ref[rows, :] + pot_ref[:, lanes] * start
        field = ((image - center * start) / half_width).astype(jnp.bfloat16)
        next_ref[:, lanes] = field
        table_ref[rows, :] = field
    pack_sends(table_ref, send_ref, nbr_ref, out_ref, count)


def second_kernel(
    nbr_ref, field_ref, own_ref, recv_ref, index_ref, ghost_index_ref, kernel_ref, scale_ref,
    pot_ref, start_ref, next_ref, energy_ref, ghost_ref, nodes_ref, product_ref, total_ref,
):
    apply_body(
        nbr_ref, field_ref, own_ref, recv_ref, index_ref, ghost_index_ref, kernel_ref,
        scale_ref, ghost_ref, nodes_ref, product_ref, total_ref,
    )
    count = field_ref.shape[0]
    energy = jnp.zeros((count, LO), jnp.float32)
    for group in range(field_ref.shape[1] // LO):
        lanes = slice(group * LO, (group + 1) * LO)
        rows = slice(group * count, (group + 1) * count)
        one = field_ref[:, lanes].astype(jnp.float32)
        start = start_ref[:, lanes].astype(jnp.float32)
        image = total_ref[rows, :] + pot_ref[:, lanes] * one
        energy = energy + one * image
        next_ref[:, lanes] = (
            2.0 * (image - center * one) / half_width - start
        ).astype(jnp.bfloat16)
    total = energy[:, :128]
    for part in range(1, LO // 128):
        total = total + energy[:, part * 128 : (part + 1) * 128]
    energy_ref[...] = total


vmem = pl.BlockSpec(memory_space=pltpu.VMEM)
smem = pl.BlockSpec(memory_space=pltpu.SMEM)
params = pltpu.CompilerParams(vmem_limit_bytes=48 << 20)


def shape(dims, kind):
    return jax.ShapeDtypeStruct(dims, kind)


def pack(neighbours, field, sends):
    count, nodes = field.shape
    return pl.pallas_call(
        pack_kernel,
        out_shape=shape((lax.axis_size("mesh"), count // 2, 128), jnp.bfloat16),
        in_specs=[smem, vmem, vmem],
        out_specs=vmem,
        scratch_shapes=[pltpu.VMEM((nodes // LO * count, LO), jnp.bfloat16)],
        compiler_params=params,
        name="pack",
    )(neighbours, field, sends)


def gather_own(field, index):
    count, nodes = field.shape
    return pl.pallas_call(
        own_kernel,
        out_shape=shape((index.shape[0], count, 128), jnp.bfloat16),
        in_specs=[vmem, vmem],
        out_specs=vmem,
        scratch_shapes=[pltpu.VMEM((nodes // LO * count, LO), jnp.bfloat16)],
        compiler_params=params,
        name="gather_own",
    )(field, index)


def apply_scratch(count, nodes, index, slots):
    return [
        pltpu.VMEM((slots // GLO * count, GLO), jnp.bfloat16),
        pltpu.VMEM((index.shape[0], count, 128), jnp.float32),
        pltpu.VMEM((index.shape[0], count, 128), jnp.float32),
        pltpu.VMEM((nodes // LO * count, LO), jnp.float32),
    ]


def first(neighbours, field, own, received, index, ghost_index, kernel, scale, pot, sends):
    count, nodes = field.shape
    return pl.pallas_call(
        first_kernel,
        out_shape=(
            shape(field.shape, jnp.bfloat16),
            shape((lax.axis_size("mesh"), count // 2, 128), jnp.bfloat16),
        ),
        in_specs=[smem] + [vmem] * 9,
        out_specs=(vmem, vmem),
        scratch_shapes=[pltpu.VMEM((nodes // LO * count, LO), jnp.bfloat16)]
        + apply_scratch(count, nodes, index, sends.size),
        compiler_params=params,
        name="first",
    )(neighbours, field, own, received, index, ghost_index, kernel, scale, pot, sends)


def second(neighbours, field, own, received, index, ghost_index, kernel, scale, pot, start, slots):
    count, nodes = field.shape
    return pl.pallas_call(
        second_kernel,
        out_shape=(shape(field.shape, jnp.bfloat16), shape((count, 128), jnp.float32)),
        in_specs=[smem] + [vmem] * 9,
        out_specs=(vmem, vmem),
        scratch_shapes=apply_scratch(count, nodes, index, slots),
        compiler_params=params,
        name="second",
    )(neighbours, field, own, received, index, ghost_index, kernel, scale, pot, start)


def swap(value, axis):
    return lax.all_to_all(value, axis, split_axis=0, concat_axis=0, tiled=True)


def prepare(cell_map, neighbours, nodes, slot_count):
    npe, cells = cell_map.shape
    pad = -npe % STEP
    owner = (cell_map - nodes) // slot_count
    position = jnp.zeros_like(cell_map)
    for place in range(neighbours.shape[0]):
        position = jnp.where(owner == neighbours[place], place, position)
    ghost = position * slot_count + (cell_map - nodes) % slot_count
    own = cell_map < nodes
    own_index = jnp.where(own, cell_map, -1)
    ghost_index = jnp.where(own, -1, ghost)
    fill = ((0, pad), (0, 0))
    return (
        jnp.pad(own_index, fill, constant_values=-1),
        jnp.pad(ghost_index, fill, constant_values=-1),
    )


def per_device(
    filter_block,
    local_pot,
    cell_scale,
    cell_kernel,
    cell_map,
    neighbour_ids,
    send_nodes,
    rotation_rows,
    panel_owner,
):
    count, node_count = filter_block.shape
    mesh_size = lax.axis_size("mesh")
    band_size = lax.axis_size("band")
    neighbours = neighbour_ids[0]
    slots = send_nodes.shape[2]
    sends = send_nodes.reshape(-1, 128)
    pot = local_pot.reshape(1, -1)
    scale = cell_scale.reshape(1, -1)
    outgoing = pack(neighbours, filter_block, sends)
    incoming = swap(outgoing, "mesh")
    all_rows = swap(jnp.broadcast_to(rotation_rows, (band_size,) + rotation_rows.shape), "band")
    index, ghost_index = prepare(cell_map, neighbours, node_count, slots)
    pad = index.shape[0] - cell_kernel.shape[0]
    kernel = jnp.pad(cell_kernel, ((0, pad), (0, pad)))
    own = gather_own(filter_block, index)
    field_one, outgoing = first(
        neighbours, filter_block, own, incoming, index, ghost_index, kernel, scale, pot, sends
    )
    incoming = swap(outgoing, "mesh")
    own = gather_own(field_one, index)
    filtered, energy = second(
        neighbours, field_one, own, incoming, index, ghost_index, kernel, scale, pot,
        filter_block, sends.size,
    )
    width = node_count // band_size
    parts = filtered.reshape(count, band_size, width).transpose(1, 0, 2)
    states = swap(parts, "band")
    energy_local = jnp.sum(energy, axis=1)
    gathered = swap(jnp.broadcast_to(energy_local, (mesh_size, 1, count)), "mesh")
    state_energy = jnp.sum(gathered[:, 0, :], axis=0) / (node_count * mesh_size)
    panels = jnp.take(states, panel_owner, axis=0).reshape(-1, width)
    coefficients = jnp.take(all_rows, panel_owner, axis=0).reshape(-1, rotation_rows.shape[1])
    rotated = lax.dot_general(
        coefficients, panels, (((0,), (0,)), ((), ())), preferred_element_type=jnp.float32
    ).astype(jnp.bfloat16)
    return (filtered, rotated, state_energy)


def solution(mesh):
    placed = (
        P("band", "mesh"),
        P("mesh"),
        P("mesh"),
        P(),
        P(None, "mesh"),
        P("mesh", None),
        P("mesh", None, None),
        P("band", None),
        P(),
    )
    return jax.shard_map(
        per_device,
        mesh=mesh,
        in_specs=placed,
        out_specs=(P("band", "mesh"), P(None, ("mesh", "band")), P("band")),
        check_vma=False,
    )
```

```python
import jax
import jax.numpy as jnp
from jax import lax
from jax.experimental import pallas as pl
from jax.experimental.pallas import tpu as pltpu
from jax.sharding import PartitionSpec as P

center = 6.0
half_width = 4.0
LO = 512
GLO = 128
STEP = 8


def chunks(total):
    return [(base, min(STEP, total - base)) for base in range(0, total, STEP)]


def flags(row, width):
    parts = []
    level = lax.broadcasted_iota(jnp.int32, (min(width, 256), 128), 0)
    level = level.astype(jnp.float32).astype(jnp.bfloat16)
    one = jnp.ones(level.shape, jnp.bfloat16)
    zero = jnp.zeros(level.shape, jnp.bfloat16)
    for base in range(0, width, level.shape[0]):
        local = row - base
        local = jnp.where((local >= 0) & (local < level.shape[0]), local, -1)
        local = local.astype(jnp.float32).astype(jnp.bfloat16)
        parts.append(jnp.where(level == jnp.broadcast_to(local, level.shape), one, zero))
    return parts[0] if len(parts) == 1 else jnp.concatenate(parts, axis=0)


def low_part(row, width):
    return jnp.bitwise_and(row, width - 1)


def high_part(row, width):
    return jnp.right_shift(row, width.bit_length() - 1)


def choose(product, highs, count):
    groups = product.shape[0] // count
    picked = []
    for k, high in enumerate(highs):
        total = jnp.zeros((count, 128), jnp.float32)
        for group in range(groups):
            part = product[group * count : (group + 1) * count, k * 128 : (k + 1) * 128]
            total = jnp.where(high == group, part, total)
        picked.append(total)
    return picked


def row_list(block):
    return [block[k : k + 1, :] for k in range(block.shape[0])]


def stack_groups(field_ref, table_ref, count):
    for group in range(field_ref.shape[1] // LO):
        table_ref[group * count : (group + 1) * count, :] = field_ref[
            :, group * LO : (group + 1) * LO
        ]


def pack_sends(table_ref, send_ref, nbr_ref, out_ref, count):
    out_ref[...] = jnp.zeros(out_ref.shape, out_ref.dtype)
    rows = row_list(send_ref[...])
    marks = jnp.concatenate([flags(low_part(row, LO), LO) for row in rows], axis=1)
    product = jnp.dot(table_ref[...], marks, preferred_element_type=jnp.float32)
    picked = choose(product, [high_part(row, LO) for row in rows], count)
    half = count // 2
    for k, part in enumerate(picked):
        for side in range(2):
            block = part[:, side * 64 : (side + 1) * 64]
            tile = jnp.concatenate([block[:half], block[half:]], axis=1)
            out_ref[nbr_ref[2 * k + side]] = tile.astype(jnp.bfloat16)


def pack_kernel(nbr_ref, field_ref, send_ref, out_ref, table_ref):
    count = field_ref.shape[0]
    stack_groups(field_ref, table_ref, count)
    pack_sends(table_ref, send_ref, nbr_ref, out_ref, count)


def gather_chunk(table, map_ref, marks, own_ref, base, size, count):
    product = jnp.dot(table, marks, preferred_element_type=jnp.float32)
    rows = row_list(map_ref[base : base + size, :])
    for k, part in enumerate(choose(product, [high_part(row, LO) for row in rows], count)):
        own_ref[base + k] = part.astype(jnp.bfloat16)


def build_kernel(nbr_ref, field_ref, map_ref, own_ref, mark_ref, ghost_mark_ref, high_ref, table_ref):
    count, nodes = field_ref.shape
    stack_groups(field_ref, table_ref, count)
    for base, size in chunks(map_ref.shape[0]):
        block = map_ref[base : base + size, :]
        marks = jnp.concatenate([flags(low_part(row, LO), LO) for row in row_list(block)], axis=1)
        lanes = slice(base * 128, (base + size) * 128)
        mark_ref[:, lanes] = marks
        gather_chunk(table_ref[...], map_ref, marks, own_ref, base, size, count)
        slot = block - nodes
        owner = jnp.right_shift(slot, 6)
        place = jnp.full(block.shape, -1, jnp.int32)
        for position in range(nbr_ref.shape[0]):
            place = jnp.where(owner == nbr_ref[position], position, place)
        compact = jnp.where(place >= 0, place * 64 + jnp.bitwise_and(slot, 63), -1)
        high_ref[base : base + size, :] = high_part(compact, GLO)
        ghost_mark_ref[:, lanes] = jnp.concatenate(
            [flags(low_part(row, GLO), GLO) for row in row_list(compact)], axis=1
        )


def gather_kernel(field_ref, map_ref, mark_ref, own_ref, table_ref):
    count = field_ref.shape[0]
    stack_groups(field_ref, table_ref, count)
    for base, size in chunks(map_ref.shape[0]):
        marks = mark_ref[:, base * 128 : (base + size) * 128]
        gather_chunk(table_ref[...], map_ref, marks, own_ref, base, size, count)


def contract(
    nbr_ref, own_ref, recv_ref, high_ref, ghost_mark_ref, kernel_ref, scale_ref,
    ghost_ref, square_ref, nodes_ref, product_ref,
):
    npe, count, _ = own_ref.shape
    half = count // 2
    for k in range(ghost_ref.shape[0] // count):
        left = recv_ref[nbr_ref[2 * k]]
        right = recv_ref[nbr_ref[2 * k + 1]]
        ghost_ref[k * count : k * count + half, :] = jnp.concatenate(
            [left[:, :64], right[:, :64]], axis=1
        )
        ghost_ref[k * count + half : (k + 1) * count, :] = jnp.concatenate(
            [left[:, 64:], right[:, 64:]], axis=1
        )
    for base, size in chunks(npe):
        marks = ghost_mark_ref[:, base * 128 : (base + size) * 128]
        product = jnp.dot(ghost_ref[...], marks, preferred_element_type=jnp.float32)
        rows = row_list(high_ref[base : base + size, :])
        for k, part in enumerate(choose(product, rows, count)):
            nodes_ref[base + k] = part + own_ref[base + k].astype(jnp.float32)
    square_ref[...] = jnp.zeros(square_ref.shape, square_ref.dtype)
    square_ref[:npe, :npe] = kernel_ref[...]
    nodes_ref[npe:] = jnp.zeros((nodes_ref.shape[0] - npe,) + nodes_ref.shape[1:], jnp.float32)
    scale = scale_ref[...]
    for state in range(0, count, 2):
        columns = jnp.concatenate(
            [nodes_ref[:, state, :], nodes_ref[:, state + 1, :]], axis=1
        ).astype(jnp.bfloat16)
        product = jnp.dot(square_ref[...], columns, preferred_element_type=jnp.float32)
        product_ref[:, state, :] = product[:, :128] * scale
        product_ref[:, state + 1, :] = product[:, 128:] * scale


def scatter(map_ref, mark_ref, product_ref, total_ref, count):
    groups = total_ref.shape[0] // count
    zero = jnp.zeros((count, 128), jnp.bfloat16)
    for base, size in chunks(map_ref.shape[0]):
        parts = []
        for k, row in enumerate(row_list(map_ref[base : base + size, :])):
            high = high_part(row, LO).astype(jnp.float32).astype(jnp.bfloat16)
            high = jnp.broadcast_to(high, zero.shape)
            value = product_ref[base + k].astype(jnp.bfloat16)
            parts.append(
                jnp.concatenate(
                    [
                        jnp.where(high == jnp.full(zero.shape, group, jnp.bfloat16), value, zero)
                        for group in range(groups)
                    ],
                    axis=0,
                )
            )
        marks = mark_ref[:, base * 128 : (base + size) * 128]
        sums = lax.dot_general(
            jnp.concatenate(parts, axis=1), marks, (((1,), (1,)), ((), ())),
            preferred_element_type=jnp.float32,
        )
        if base == 0:
            total_ref[...] = sums
        else:
            total_ref[...] += sums


def first_kernel(
    nbr_ref, field_ref, own_ref, recv_ref, map_ref, mark_ref, high_ref, ghost_mark_ref,
    kernel_ref, scale_ref, pot_ref, send_ref,
    next_ref, out_ref, table_ref, ghost_ref, square_ref, nodes_ref, product_ref, total_ref,
):
    count = field_ref.shape[0]
    contract(
        nbr_ref, own_ref, recv_ref, high_ref, ghost_mark_ref, kernel_ref, scale_ref,
        ghost_ref, square_ref, nodes_ref, product_ref,
    )
    scatter(map_ref, mark_ref, product_ref, total_ref, count)
    for group in range(field_ref.shape[1] // LO):
        lanes = slice(group * LO, (group + 1) * LO)
        rows = slice(group * count, (group + 1) * count)
        start = field_ref[:, lanes].astype(jnp.float32)
        image = total_ref[rows, :] + pot_ref[:, lanes] * start
        field = ((image - center * start) / half_width).astype(jnp.bfloat16)
        next_ref[:, lanes] = field
        table_ref[rows, :] = field
    pack_sends(table_ref, send_ref, nbr_ref, out_ref, count)


def energy_kernel(
    nbr_ref, field_ref, own_ref, recv_ref, high_ref, ghost_mark_ref, kernel_ref, scale_ref,
    pot_ref, cells_ref, energy_ref, ghost_ref, square_ref, nodes_ref, product_ref,
):
    count, nodes = field_ref.shape
    contract(
        nbr_ref, own_ref, recv_ref, high_ref, ghost_mark_ref, kernel_ref, scale_ref,
        ghost_ref, square_ref, nodes_ref, product_ref,
    )
    total = jnp.zeros((count, 128), jnp.float32)
    for base in range(own_ref.shape[0]):
        value = product_ref[base]
        cells_ref[base] = value.astype(jnp.bfloat16)
        total = total + value * own_ref[base].astype(jnp.float32)
    for base in range(0, nodes, 128):
        one = field_ref[:, base : base + 128].astype(jnp.float32)
        total = total + pot_ref[:, base : base + 128] * one * one
    sums = jnp.broadcast_to(jnp.sum(total, axis=1, keepdims=True), total.shape)
    state = lax.broadcasted_iota(jnp.int32, total.shape, 0)
    lane = lax.broadcasted_iota(jnp.int32, total.shape, 1)
    line = jnp.sum(jnp.where(state == lane, sums, 0.0), axis=0, keepdims=True)
    energy_ref[...] = jnp.broadcast_to(line[None], energy_ref.shape)


def second_kernel(
    field_ref, cells_ref, map_ref, mark_ref, pot_ref, start_ref, next_ref, out_ref, total_ref
):
    count = field_ref.shape[0]
    scatter(map_ref, mark_ref, cells_ref, total_ref, count)
    for group in range(field_ref.shape[1] // LO):
        lanes = slice(group * LO, (group + 1) * LO)
        rows = slice(group * count, (group + 1) * count)
        one = field_ref[:, lanes].astype(jnp.float32)
        start = start_ref[:, lanes].astype(jnp.float32)
        image = total_ref[rows, :] + pot_ref[:, lanes] * one
        next_ref[:, lanes] = (
            2.0 * (image - center * one) / half_width - start
        ).astype(jnp.bfloat16)
    width = out_ref.shape[2]
    for band in range(out_ref.shape[0]):
        out_ref[band] = next_ref[:, band * width : (band + 1) * width]


def rotate_kernel(owner_ref, rows_ref, states_ref, out_ref):
    coefficients = [rows_ref[owner_ref[k]] for k in range(owner_ref.shape[0])]
    panels = [states_ref[owner_ref[k]] for k in range(owner_ref.shape[0])]
    out_ref[...] = lax.dot_general(
        jnp.concatenate(coefficients, axis=0),
        jnp.concatenate(panels, axis=0),
        (((0,), (0,)), ((), ())),
        preferred_element_type=jnp.float32,
    ).astype(jnp.bfloat16)


vmem = pl.BlockSpec(memory_space=pltpu.VMEM)
smem = pl.BlockSpec(memory_space=pltpu.SMEM)


def call(kernel, name, outs, scratch, scalar, *operands):
    return pl.pallas_call(
        kernel,
        out_shape=tuple(jax.ShapeDtypeStruct(dims, kind) for dims, kind in outs),
        in_specs=[smem] * scalar + [vmem] * (len(operands) - scalar),
        out_specs=tuple(vmem for _ in outs),
        scratch_shapes=[pltpu.VMEM(dims, kind) for dims, kind in scratch],
        compiler_params=pltpu.CompilerParams(vmem_limit_bytes=LIMIT),
        name=name,
    )(*operands)


LIMIT = 20 << 20
half = jnp.bfloat16
full = jnp.float32


def swap(value, axis):
    return lax.all_to_all(value, axis, split_axis=0, concat_axis=0, tiled=True)


def per_device(
    filter_block,
    local_pot,
    cell_scale,
    cell_kernel,
    cell_map,
    neighbour_ids,
    send_nodes,
    rotation_rows,
    panel_owner,
):
    count, nodes = filter_block.shape
    npe, cells = cell_map.shape
    mesh_size = lax.axis_size("mesh")
    band_size = lax.axis_size("band")
    neighbours = neighbour_ids[0]
    sends = send_nodes.reshape(-1, 128)
    pot = local_pot.reshape(1, -1)
    scale = cell_scale.reshape(1, -1)
    table = ((nodes // LO * count, LO), half)
    total = ((nodes // LO * count, LO), full)
    outbox = ((mesh_size, count // 2, 128), half)
    columns = ((npe, count, cells), half)
    padded = npe + -npe % 8
    inner = [
        ((send_nodes.size // GLO * count, GLO), half),
        ((padded, padded), half),
        ((padded, count, cells), full),
        ((padded, count, cells), full),
    ]

    (outgoing,) = call(pack_kernel, "pack", [outbox], [table], 1, neighbours, filter_block, sends)
    incoming = swap(outgoing, "mesh")
    own, marks, ghost_marks, highs = call(
        build_kernel, "build",
        [columns, ((LO, npe * cells), half), ((GLO, npe * cells), half), ((npe, cells), jnp.int32)],
        [table], 1, neighbours, filter_block, cell_map,
    )
    field_one, outgoing = call(
        first_kernel, "first", [((count, nodes), half), outbox], [table] + inner + [total], 1,
        neighbours, filter_block, own, incoming, cell_map, marks, highs, ghost_marks,
        cell_kernel, scale, pot, sends,
    )
    incoming = swap(outgoing, "mesh")
    (own,) = call(gather_kernel, "gather", [columns], [table], 0, field_one, cell_map, marks)
    all_rows = swap(jnp.broadcast_to(rotation_rows, (band_size,) + rotation_rows.shape), "band")
    products, energy = call(
        energy_kernel, "energy", [columns, ((mesh_size, 1, 128), full)], inner, 1,
        neighbours, field_one, own, incoming, highs, ghost_marks, cell_kernel, scale, pot,
    )
    energies = swap(energy, "mesh")
    filtered, parts = call(
        second_kernel, "second",
        [((count, nodes), half), ((band_size, count, nodes // band_size), half)], [total], 0,
        field_one, products, cell_map, marks, pot, filter_block,
    )
    parts, all_rows, energies = lax.optimization_barrier((parts, all_rows, energies))
    states = swap(parts, "band")
    state_energy = jnp.sum(energies[:, 0, :count], axis=0) / (nodes * mesh_size)
    (rotated,) = call(
        rotate_kernel, "rotate", [((rotation_rows.shape[1], nodes // band_size), half)], [], 1,
        panel_owner, all_rows, states,
    )
    return (filtered, rotated, state_energy)


def solution(mesh):
    placed = (
        P("band", "mesh"),
        P("mesh"),
        P("mesh"),
        P(),
        P(None, "mesh"),
        P("mesh", None),
        P("mesh", None, None),
        P("band", None),
        P(),
    )
    return jax.shard_map(
        per_device,
        mesh=mesh,
        in_specs=placed,
        out_specs=(P("band", "mesh"), P(None, ("mesh", "band")), P("band")),
        check_vma=False,
    )
```

```python
import jax
import jax.numpy as jnp
from jax import lax
from jax.experimental import pallas as pl
from jax.experimental.pallas import tpu as pltpu
from jax.sharding import PartitionSpec as P

center = 6.0
half_width = 4.0
LO = 512
GLO = 128
STEP = 8
UNROLL = 4


def sweep(steps, body):
    def group(number, carry):
        for place in range(UNROLL):
            body(number * UNROLL + place)
        return carry

    lax.fori_loop(0, steps // UNROLL, group, 0)


def flags(row, width):
    parts = []
    level = lax.broadcasted_iota(jnp.int32, (min(width, 256), 128), 0)
    level = level.astype(jnp.float32).astype(jnp.bfloat16)
    one = jnp.ones(level.shape, jnp.bfloat16)
    zero = jnp.zeros(level.shape, jnp.bfloat16)
    for base in range(0, width, level.shape[0]):
        local = row - base
        local = jnp.where((local >= 0) & (local < level.shape[0]), local, -1)
        local = local.astype(jnp.float32).astype(jnp.bfloat16)
        parts.append(jnp.where(level == jnp.broadcast_to(local, level.shape), one, zero))
    return parts[0] if len(parts) == 1 else jnp.concatenate(parts, axis=0)


def low_part(row, width):
    return jnp.bitwise_and(row, width - 1)


def high_part(row, width):
    return jnp.right_shift(row, width.bit_length() - 1)


def choose(product, highs, count):
    groups = product.shape[0] // count
    picked = []
    for k, high in enumerate(highs):
        total = jnp.zeros((count, 128), jnp.float32)
        for group in range(groups):
            part = product[group * count : (group + 1) * count, k * 128 : (k + 1) * 128]
            total = jnp.where(high == group, part, total)
        picked.append(total)
    return picked


def row_list(block):
    return [block[k : k + 1, :] for k in range(block.shape[0])]


def stack_groups(field_ref, table_ref, count):
    for group in range(field_ref.shape[1] // LO):
        table_ref[group * count : (group + 1) * count, :] = field_ref[
            :, group * LO : (group + 1) * LO
        ]


class Copies:
    def __init__(self, sems):
        self.sems = sems
        self.used = 0

    def start(self, source, target):
        copy = pltpu.make_async_copy(source, target, self.sems.at[self.used])
        copy.start()
        self.used += 1
        return copy


def marks_of(block, width):
    return jnp.concatenate([flags(low_part(row, width), width) for row in row_list(block)], axis=1)


def read_map(copies, map_hbm, map_ref):
    npe = map_hbm.shape[0]
    return copies.start(map_hbm, map_ref.at[:npe])


def fill_map(map_ref, npe):
    rest = map_ref.shape[0] - npe
    map_ref[npe:, :] = jnp.full((rest, map_ref.shape[1]), -1, jnp.int32)


def block_of(ref, number):
    return ref[pl.ds(pl.multiple_of(number * STEP, STEP), STEP), :]


def pack_sends(table_ref, send_ref, nbr_ref, out_ref, count):
    out_ref[...] = jnp.zeros(out_ref.shape, out_ref.dtype)
    rows = [
        jnp.concatenate([send_ref[k], send_ref[k + 1]], axis=1)
        for k in range(0, send_ref.shape[0], 2)
    ]
    marks = jnp.concatenate([flags(low_part(row, LO), LO) for row in rows], axis=1)
    product = jnp.dot(table_ref[...], marks, preferred_element_type=jnp.float32)
    picked = choose(product, [high_part(row, LO) for row in rows], count)
    half = count // 2
    for k, part in enumerate(picked):
        for side in range(2):
            block = part[:, side * 64 : (side + 1) * 64]
            tile = jnp.concatenate([block[:half], block[half:]], axis=1)
            out_ref[nbr_ref[0, 2 * k + side]] = tile.astype(jnp.bfloat16)


def pack_kernel(
    nbr_hbm, field_hbm, send_hbm, out_hbm, field_ref, send_ref, table_ref, out_ref, nbr_ref, sems
):
    copies = Copies(sems)
    nbr_copy = copies.start(nbr_hbm, nbr_ref)
    field_copy = copies.start(field_hbm, field_ref)
    send_copy = copies.start(send_hbm, send_ref)
    count = field_ref.shape[0]
    field_copy.wait()
    stack_groups(field_ref, table_ref, count)
    send_copy.wait()
    nbr_copy.wait()
    pack_sends(table_ref, send_ref, nbr_ref, out_ref, count)
    copies.start(out_ref, out_hbm).wait()


def gather_chunk(table, block, marks, own_ref, number, count):
    product = jnp.dot(table, marks, preferred_element_type=jnp.float32)
    highs = [high_part(row, LO) for row in row_list(block)]
    for k, part in enumerate(choose(product, highs, count)):
        own_ref[number * STEP + k] = part.astype(jnp.bfloat16)


def gather_kernel(field_hbm, map_hbm, rows_hbm, own_hbm, copies_hbm, field_ref, map_ref, rows_ref, own_ref, table_ref, sems):
    copies = Copies(sems)
    field_copy = copies.start(field_hbm, field_ref)
    map_copy = read_map(copies, map_hbm, map_ref)
    rows_copy = copies.start(rows_hbm, rows_ref)
    count = field_ref.shape[0]
    field_copy.wait()
    stack_groups(field_ref, table_ref, count)
    rows_copy.wait()
    pending = [copies.start(rows_ref, copies_hbm.at[k]) for k in range(copies_hbm.shape[0])]
    map_copy.wait()
    fill_map(map_ref, map_hbm.shape[0])

    def body(number):
        block = block_of(map_ref, number)
        gather_chunk(table_ref[...], block, marks_of(block, LO), own_ref, number, count)

    sweep(map_ref.shape[0] // STEP, body)
    copies.start(own_ref, own_hbm).wait()
    for copy in pending:
        copy.wait()


def contract(
    copies, nbr_hbm, own_hbm, recv_hbm, map_hbm, kernel_hbm, scale_hbm,
    own_ref, recv_ref, map_ref, kernel_ref, scale_ref,
    ghost_ref, square_ref, nodes_ref, product_ref, nbr_ref, nodes, later,
):
    count = own_ref.shape[1]
    npe = kernel_hbm.shape[0]
    half = count // 2
    nbr_copy = copies.start(nbr_hbm, nbr_ref)
    recv_copy = copies.start(recv_hbm, recv_ref)
    map_copy = read_map(copies, map_hbm, map_ref)
    own_copy = copies.start(own_hbm, own_ref)
    kernel_copy = copies.start(kernel_hbm, kernel_ref)
    scale_copy = copies.start(scale_hbm, scale_ref)
    rest = later()
    square_ref[...] = jnp.zeros(square_ref.shape, square_ref.dtype)
    nbr_copy.wait()
    neighbours = [nbr_ref[0, position] for position in range(nbr_ref.shape[1])]
    recv_copy.wait()
    for k in range(ghost_ref.shape[0] // count):
        left = recv_ref[neighbours[2 * k]]
        right = recv_ref[neighbours[2 * k + 1]]
        ghost_ref[k * count : k * count + half, :] = jnp.concatenate(
            [left[:, :64], right[:, :64]], axis=1
        )
        ghost_ref[k * count + half : (k + 1) * count, :] = jnp.concatenate(
            [left[:, 64:], right[:, 64:]], axis=1
        )
    map_copy.wait()
    fill_map(map_ref, map_hbm.shape[0])
    own_copy.wait()

    def body(number):
        slot = block_of(map_ref, number) - nodes
        owner = jnp.right_shift(slot, 6)
        place = jnp.full(slot.shape, -1, jnp.int32)
        for position, neighbour in enumerate(neighbours):
            place = jnp.where(owner == neighbour, position, place)
        compact = jnp.where(place >= 0, place * 64 + jnp.bitwise_and(slot, 63), -1)
        product = jnp.dot(
            ghost_ref[...], marks_of(compact, GLO), preferred_element_type=jnp.float32
        )
        highs = [high_part(row, GLO) for row in row_list(compact)]
        for k, part in enumerate(choose(product, highs, count)):
            base = number * STEP + k
            nodes_ref[base] = part + own_ref[base].astype(jnp.float32)

    sweep(map_ref.shape[0] // STEP, body)
    kernel_copy.wait()
    square_ref[:npe, :npe] = kernel_ref[...]
    scale_copy.wait()
    scale = scale_ref[...]
    for state in range(0, count, 2):
        columns = jnp.concatenate(
            [nodes_ref[:, state, :], nodes_ref[:, state + 1, :]], axis=1
        ).astype(jnp.bfloat16)
        product = jnp.dot(square_ref[...], columns, preferred_element_type=jnp.float32)
        product_ref[:, state, :] = product[:, :128] * scale
        product_ref[:, state + 1, :] = product[:, 128:] * scale
    return rest


def scatter(map_ref, product_ref, total_ref, count):
    groups = total_ref.shape[0] // count
    zero = jnp.zeros((count, 128), jnp.bfloat16)
    total_ref[...] = jnp.zeros(total_ref.shape, jnp.float32)

    def body(number):
        block = block_of(map_ref, number)
        parts = []
        for k, row in enumerate(row_list(block)):
            high = high_part(row, LO).astype(jnp.float32).astype(jnp.bfloat16)
            high = jnp.broadcast_to(high, zero.shape)
            value = product_ref[number * STEP + k].astype(jnp.bfloat16)
            parts.append(
                jnp.concatenate(
                    [
                        jnp.where(high == jnp.full(zero.shape, group, jnp.bfloat16), value, zero)
                        for group in range(groups)
                    ],
                    axis=0,
                )
            )
        total_ref[...] += lax.dot_general(
            jnp.concatenate(parts, axis=1), marks_of(block, LO), (((1,), (1,)), ((), ())),
            preferred_element_type=jnp.float32,
        )

    sweep(map_ref.shape[0] // STEP, body)


def first_kernel(
    nbr_hbm, own_hbm, recv_hbm, map_hbm, kernel_hbm, scale_hbm, field_hbm, pot_hbm, send_hbm,
    next_hbm, out_hbm,
    own_ref, recv_ref, map_ref, kernel_ref, scale_ref,
    ghost_ref, square_ref, nodes_ref, product_ref,
    field_ref, pot_ref, send_ref, next_ref, table_ref, total_ref, out_ref,
    nbr_ref, sems,
):
    copies = Copies(sems)
    count, nodes = field_ref.shape

    def later():
        return [
            copies.start(field_hbm, field_ref),
            copies.start(pot_hbm, pot_ref),
            copies.start(send_hbm, send_ref),
        ]

    others = contract(
        copies, nbr_hbm, own_hbm, recv_hbm, map_hbm, kernel_hbm, scale_hbm,
        own_ref, recv_ref, map_ref, kernel_ref, scale_ref,
        ghost_ref, square_ref, nodes_ref, product_ref, nbr_ref, nodes, later,
    )
    scatter(map_ref, product_ref, total_ref, count)
    for copy in others:
        copy.wait()
    for group in range(field_ref.shape[1] // LO):
        lanes = slice(group * LO, (group + 1) * LO)
        rows = slice(group * count, (group + 1) * count)
        start = field_ref[:, lanes].astype(jnp.float32)
        image = total_ref[rows, :] + pot_ref[:, lanes] * start
        field = ((image - center * start) / half_width).astype(jnp.bfloat16)
        next_ref[:, lanes] = field
        table_ref[rows, :] = field
    next_copy = copies.start(next_ref, next_hbm)
    pack_sends(table_ref, send_ref, nbr_ref, out_ref, count)
    copies.start(out_ref, out_hbm).wait()
    next_copy.wait()


def energy_kernel(
    nbr_hbm, own_hbm, recv_hbm, map_hbm, kernel_hbm, scale_hbm, field_hbm, pot_hbm,
    cells_hbm, energy_ref,
    own_ref, recv_ref, map_ref, kernel_ref, scale_ref,
    ghost_ref, square_ref, nodes_ref, product_ref, field_ref, pot_ref, cells_ref, nbr_ref, sems,
):
    copies = Copies(sems)
    count, nodes = field_ref.shape

    def later():
        return [copies.start(field_hbm, field_ref), copies.start(pot_hbm, pot_ref)]

    others = contract(
        copies, nbr_hbm, own_hbm, recv_hbm, map_hbm, kernel_hbm, scale_hbm,
        own_ref, recv_ref, map_ref, kernel_ref, scale_ref,
        ghost_ref, square_ref, nodes_ref, product_ref, nbr_ref, nodes, later,
    )
    total = jnp.zeros((count, 128), jnp.float32)
    for base in range(own_ref.shape[0]):
        value = product_ref[base]
        cells_ref[base] = value.astype(jnp.bfloat16)
        total = total + value * own_ref[base].astype(jnp.float32)
    cells_copy = copies.start(cells_ref, cells_hbm)
    for copy in others:
        copy.wait()
    for base in range(0, nodes, 128):
        one = field_ref[:, base : base + 128].astype(jnp.float32)
        total = total + pot_ref[:, base : base + 128] * one * one
    sums = jnp.broadcast_to(jnp.sum(total, axis=1, keepdims=True), total.shape)
    state = lax.broadcasted_iota(jnp.int32, total.shape, 0)
    lane = lax.broadcasted_iota(jnp.int32, total.shape, 1)
    line = jnp.sum(jnp.where(state == lane, sums, 0.0), axis=0, keepdims=True)
    energy_ref[...] = jnp.broadcast_to(line[None], energy_ref.shape)
    cells_copy.wait()


def second_kernel(
    field_hbm, cells_hbm, map_hbm, pot_hbm, start_hbm, next_hbm, out_hbm,
    field_ref, cells_ref, map_ref, pot_ref, start_ref, next_ref, total_ref, sems,
):
    copies = Copies(sems)
    count = field_ref.shape[0]
    map_copy = read_map(copies, map_hbm, map_ref)
    cell_copy = copies.start(cells_hbm, cells_ref)
    others = [
        copies.start(field_hbm, field_ref),
        copies.start(pot_hbm, pot_ref),
        copies.start(start_hbm, start_ref),
    ]
    map_copy.wait()
    fill_map(map_ref, map_hbm.shape[0])
    cell_copy.wait()
    scatter(map_ref, cells_ref, total_ref, count)
    for copy in others:
        copy.wait()
    for group in range(field_ref.shape[1] // LO):
        lanes = slice(group * LO, (group + 1) * LO)
        rows = slice(group * count, (group + 1) * count)
        one = field_ref[:, lanes].astype(jnp.float32)
        start = start_ref[:, lanes].astype(jnp.float32)
        image = total_ref[rows, :] + pot_ref[:, lanes] * one
        next_ref[:, lanes] = (
            2.0 * (image - center * one) / half_width - start
        ).astype(jnp.bfloat16)
    width = out_hbm.shape[2]
    pending = [copies.start(next_ref, next_hbm)]
    for band in range(out_hbm.shape[0]):
        pending.append(
            copies.start(next_ref.at[:, band * width : (band + 1) * width], out_hbm.at[band])
        )
    for copy in pending:
        copy.wait()


def rotate_kernel(owner_hbm, rows_hbm, states_hbm, out_hbm, rows_ref, states_ref, out_ref, owner_ref, sems):
    copies = Copies(sems)
    copies.start(owner_hbm, owner_ref).wait()
    pending = []
    count = rows_hbm.shape[1]
    for k in range(owner_ref.shape[0]):
        place = pl.ds(k * count, count)
        pending.append(copies.start(rows_hbm.at[owner_ref[k]], rows_ref.at[place]))
        pending.append(copies.start(states_hbm.at[owner_ref[k]], states_ref.at[place]))
    for copy in pending:
        copy.wait()
    out_ref[...] = lax.dot_general(
        rows_ref[...], states_ref[...], (((0,), (0,)), ((), ())),
        preferred_element_type=jnp.float32,
    ).astype(jnp.bfloat16)
    copies.start(out_ref, out_hbm).wait()


vmem = pl.BlockSpec(memory_space=pltpu.VMEM)
hbm = pl.BlockSpec(memory_space=pltpu.HBM)
anywhere = pl.BlockSpec(memory_space=pl.ANY)
half = jnp.bfloat16
full = jnp.float32
whole = jnp.int32


def call(kernel, name, outs, scratch, scalars, sems, *operands, free=-1):
    held = [
        value if k == free else pltpu.with_memory_space_constraint(value, pltpu.HBM)
        for k, value in enumerate(operands)
    ]
    return pl.pallas_call(
        kernel,
        out_shape=tuple(
            jax.ShapeDtypeStruct(dims, kind) if place is vmem else pltpu.HBM(dims, kind)
            for dims, kind, place in outs
        ),
        in_specs=[anywhere if k == free else hbm for k in range(len(operands))],
        out_specs=tuple(place for _, _, place in outs),
        scratch_shapes=[pltpu.VMEM(dims, kind) for dims, kind in scratch]
        + [pltpu.SMEM(dims, jnp.int32) for dims in scalars]
        + [pltpu.SemaphoreType.DMA((sems,))],
        compiler_params=pltpu.CompilerParams(vmem_limit_bytes=48 << 20),
        name=name,
    )(*held)


def swap(value, axis):
    return lax.all_to_all(value, axis, split_axis=0, concat_axis=0, tiled=True)


def per_device(
    filter_block,
    local_pot,
    cell_scale,
    cell_kernel,
    cell_map,
    neighbour_ids,
    send_nodes,
    rotation_rows,
    panel_owner,
):
    count, nodes = filter_block.shape
    npe, cells = cell_map.shape
    mesh_size = lax.axis_size("mesh")
    band_size = lax.axis_size("band")
    width = nodes // band_size
    sends = send_nodes.transpose(1, 0, 2)
    pot = local_pot.reshape(1, -1)
    scale = cell_scale.reshape(1, -1)
    steps = -(-npe // (STEP * UNROLL)) * UNROLL
    padded = steps * STEP

    field_type = ((count, nodes), half)
    map_type = ((padded, cells), whole)
    send_type = (sends.shape, whole)
    pot_type = (pot.shape, full)
    table = ((nodes // LO * count, LO), half)
    total = ((nodes // LO * count, LO), full)
    outbox = ((mesh_size, count // 2, 128), half)
    columns = ((padded, count, cells), half)
    rows_type = (rotation_rows.shape, half)
    nbr_type = neighbour_ids.shape
    inner = [
        columns, outbox, map_type, (cell_kernel.shape, half), (scale.shape, full),
        ((send_nodes.size // GLO * count, GLO), half),
        ((padded, padded), half),
        ((padded, count, cells), full),
        ((padded, count, cells), full),
    ]

    (outgoing,) = call(
        pack_kernel, "pack", [outbox + (hbm,)], [field_type, send_type, table, outbox],
        [nbr_type], 4, neighbour_ids, filter_block, sends,
    )
    incoming = swap(outgoing, "mesh")
    copies_type = ((band_size,) + rotation_rows.shape, half)

    def gather(field):
        return call(
            gather_kernel, "gather", [columns + (hbm,), copies_type + (hbm,)],
            [field_type, map_type, rows_type, columns, table], [], 4 + band_size,
            field, cell_map, rotation_rows,
        )

    own, row_copies = gather(filter_block)
    field_one, outgoing = call(
        first_kernel, "first", [field_type + (hbm,), outbox + (hbm,)],
        inner + [field_type, pot_type, send_type, field_type, table, total, outbox],
        [nbr_type], 11, neighbour_ids, own, incoming, cell_map, cell_kernel, scale,
        filter_block, pot, sends, free=2,
    )
    all_rows = swap(row_copies, "band")
    outgoing, all_rows = lax.optimization_barrier((outgoing, all_rows))
    incoming = swap(outgoing, "mesh")
    own, _ = gather(field_one)
    products, energy = call(
        energy_kernel, "energy", [columns + (hbm,), ((mesh_size, 1, 128), full, vmem)],
        inner + [field_type, pot_type, columns], [nbr_type], 9,
        neighbour_ids, own, incoming, cell_map, cell_kernel, scale, field_one, pot, free=2,
    )
    energies = swap(energy, "mesh")
    filtered, parts = call(
        second_kernel, "second",
        [field_type + (hbm,), ((band_size, count, width), half, hbm)],
        [field_type, columns, map_type, pot_type, field_type, field_type, total],
        [], 6 + band_size, field_one, products, cell_map, pot, filter_block,
    )
    parts, energies = lax.optimization_barrier((parts, energies))
    states = swap(parts, "band")
    state_energy = jnp.sum(energies[:, 0, :count], axis=0) / (nodes * mesh_size)
    rotated_type = ((rotation_rows.shape[1], width), half)
    (rotated,) = call(
        rotate_kernel, "rotate", [rotated_type + (hbm,)],
        [
            ((panel_owner.size * count, rotation_rows.shape[1]), half),
            ((panel_owner.size * count, width), half),
            rotated_type,
        ],
        [panel_owner.shape], 2 + 2 * panel_owner.size, panel_owner, all_rows, states, free=2,
    )
    return (filtered, rotated, state_energy)


def solution(mesh):
    placed = (
        P("band", "mesh"),
        P("mesh"),
        P("mesh"),
        P(),
        P(None, "mesh"),
        P("mesh", None),
        P("mesh", None, None),
        P("band", None),
        P(),
    )
    return jax.shard_map(
        per_device,
        mesh=mesh,
        in_specs=placed,
        out_specs=(P("band", "mesh"), P(None, ("mesh", "band")), P("band")),
        check_vma=False,
    )
```

```python
import jax
import jax.numpy as jnp
from jax import lax
from jax.experimental import pallas as pl
from jax.experimental.pallas import tpu as pltpu
from jax.sharding import PartitionSpec as P

center = 6.0
half_width = 4.0
LO = 512
GLO = 128
STEP = 8
UNROLL = 8


def sweep(steps, body):
    def group(number, carry):
        for place in range(UNROLL):
            body(number * UNROLL + place)
        return carry

    lax.fori_loop(0, steps // UNROLL, group, 0)


def flags(row, width):
    parts = []
    level = lax.broadcasted_iota(jnp.int32, (min(width, 256), 128), 0)
    level = level.astype(jnp.float32).astype(jnp.bfloat16)
    one = jnp.ones(level.shape, jnp.bfloat16)
    zero = jnp.zeros(level.shape, jnp.bfloat16)
    for base in range(0, width, level.shape[0]):
        local = row - base
        local = jnp.where((local >= 0) & (local < level.shape[0]), local, -1)
        local = local.astype(jnp.float32).astype(jnp.bfloat16)
        parts.append(jnp.where(level == jnp.broadcast_to(local, level.shape), one, zero))
    return parts[0] if len(parts) == 1 else jnp.concatenate(parts, axis=0)


def low_part(row, width):
    return jnp.bitwise_and(row, width - 1)


def high_part(row, width):
    return jnp.right_shift(row, width.bit_length() - 1)


def choose(product, highs, count):
    groups = product.shape[0] // count
    picked = []
    for k, high in enumerate(highs):
        total = jnp.zeros((count, 128), jnp.float32)
        for group in range(groups):
            part = product[group * count : (group + 1) * count, k * 128 : (k + 1) * 128]
            total = jnp.where(high == group, part, total)
        picked.append(total)
    return picked


def row_list(block):
    return [block[k : k + 1, :] for k in range(block.shape[0])]


def stack_groups(field_ref, table_ref, count):
    for group in range(field_ref.shape[1] // LO):
        table_ref[group * count : (group + 1) * count, :] = field_ref[
            :, group * LO : (group + 1) * LO
        ]


class Copies:
    def __init__(self, sems):
        self.sems = sems
        self.used = 0

    def start(self, source, target):
        copy = pltpu.make_async_copy(source, target, self.sems.at[self.used])
        copy.start()
        self.used += 1
        return copy


def marks_of(block, width):
    return jnp.concatenate([flags(low_part(row, width), width) for row in row_list(block)], axis=1)


def read_map(copies, map_hbm, map_ref):
    npe = map_hbm.shape[0]
    return copies.start(map_hbm, map_ref.at[:npe])


def fill_map(map_ref, npe):
    rest = map_ref.shape[0] - npe
    map_ref[npe:, :] = jnp.full((rest, map_ref.shape[1]), -1, jnp.int32)


def block_of(ref, number):
    return ref[pl.ds(pl.multiple_of(number * STEP, STEP), STEP), :]


def pack_sends(table_ref, send_ref, nbr_ref, out_ref, count):
    out_ref[...] = jnp.zeros(out_ref.shape, out_ref.dtype)
    rows = [
        jnp.concatenate([send_ref[k], send_ref[k + 1]], axis=1)
        for k in range(0, send_ref.shape[0], 2)
    ]
    marks = jnp.concatenate([flags(low_part(row, LO), LO) for row in rows], axis=1)
    product = jnp.dot(table_ref[...], marks, preferred_element_type=jnp.float32)
    picked = choose(product, [high_part(row, LO) for row in rows], count)
    half = count // 2
    for k, part in enumerate(picked):
        for side in range(2):
            block = part[:, side * 64 : (side + 1) * 64]
            tile = jnp.concatenate([block[:half], block[half:]], axis=1)
            out_ref[nbr_ref[0, 2 * k + side]] = tile.astype(jnp.bfloat16)


def pack_kernel(
    nbr_hbm, owner_hbm, field_hbm, send_hbm, rows_hbm, out_hbm, panel_hbm,
    field_ref, send_ref, table_ref, rows_ref, panel_ref, out_ref, nbr_ref, owner_ref, sems,
):
    copies = Copies(sems)
    field_copy = copies.start(field_hbm, field_ref)
    send_copy = copies.start(send_hbm, send_ref)
    owner_copy = copies.start(owner_hbm, owner_ref)
    rows_copy = copies.start(rows_hbm, rows_ref)
    nbr_copy = copies.start(nbr_hbm, nbr_ref)
    count = field_ref.shape[0]
    mine = lax.axis_index("band")
    owner_copy.wait()
    rows_copy.wait()
    rows = rows_ref[...].astype(jnp.float32)
    for k in range(owner_ref.shape[0]):
        panel_ref[k * count : (k + 1) * count, :] = jnp.where(
            owner_ref[k] == mine, rows, jnp.zeros_like(rows)
        ).astype(jnp.bfloat16)
    pending = [copies.start(panel_ref, panel_hbm.at[k]) for k in range(panel_hbm.shape[0])]
    field_copy.wait()
    stack_groups(field_ref, table_ref, count)
    send_copy.wait()
    nbr_copy.wait()
    pack_sends(table_ref, send_ref, nbr_ref, out_ref, count)
    pending.append(copies.start(out_ref, out_hbm))
    for copy in pending:
        copy.wait()


def gather_chunk(table, block, marks, own_ref, number, count):
    product = jnp.dot(table, marks, preferred_element_type=jnp.float32)
    highs = [high_part(row, LO) for row in row_list(block)]
    for k, part in enumerate(choose(product, highs, count)):
        own_ref[number * STEP + k] = part.astype(jnp.bfloat16)


def gather_kernel(field_hbm, map_hbm, own_hbm, field_ref, map_ref, own_ref, table_ref, sems):
    copies = Copies(sems)
    field_copy = copies.start(field_hbm, field_ref)
    map_copy = read_map(copies, map_hbm, map_ref)
    count = field_ref.shape[0]
    field_copy.wait()
    stack_groups(field_ref, table_ref, count)
    map_copy.wait()
    fill_map(map_ref, map_hbm.shape[0])

    def body(number):
        block = block_of(map_ref, number)
        gather_chunk(table_ref[...], block, marks_of(block, LO), own_ref, number, count)

    sweep(map_ref.shape[0] // STEP, body)
    copies.start(own_ref, own_hbm).wait()


def contract(
    copies, nbr_hbm, own_hbm, recv_hbm, map_hbm, kernel_hbm, scale_hbm,
    own_ref, recv_ref, map_ref, kernel_ref, scale_ref,
    ghost_ref, square_ref, nodes_ref, product_ref, nbr_ref, nodes, later,
):
    count = own_ref.shape[1]
    npe = kernel_hbm.shape[0]
    half = count // 2
    nbr_copy = copies.start(nbr_hbm, nbr_ref)
    recv_copy = copies.start(recv_hbm, recv_ref)
    map_copy = read_map(copies, map_hbm, map_ref)
    own_copy = copies.start(own_hbm, own_ref)
    kernel_copy = copies.start(kernel_hbm, kernel_ref)
    scale_copy = copies.start(scale_hbm, scale_ref)
    rest = later()
    square_ref[...] = jnp.zeros(square_ref.shape, square_ref.dtype)
    nbr_copy.wait()
    neighbours = [nbr_ref[0, position] for position in range(nbr_ref.shape[1])]
    recv_copy.wait()
    for k in range(ghost_ref.shape[0] // count):
        left = recv_ref[neighbours[2 * k]]
        right = recv_ref[neighbours[2 * k + 1]]
        ghost_ref[k * count : k * count + half, :] = jnp.concatenate(
            [left[:, :64], right[:, :64]], axis=1
        )
        ghost_ref[k * count + half : (k + 1) * count, :] = jnp.concatenate(
            [left[:, 64:], right[:, 64:]], axis=1
        )
    map_copy.wait()
    fill_map(map_ref, map_hbm.shape[0])
    own_copy.wait()

    def body(number):
        slot = block_of(map_ref, number) - nodes
        owner = jnp.right_shift(slot, 6)
        place = jnp.full(slot.shape, -1, jnp.int32)
        for position, neighbour in enumerate(neighbours):
            place = jnp.where(owner == neighbour, position, place)
        compact = jnp.where(place >= 0, place * 64 + jnp.bitwise_and(slot, 63), -1)
        product = jnp.dot(
            ghost_ref[...], marks_of(compact, GLO), preferred_element_type=jnp.float32
        )
        highs = [high_part(row, GLO) for row in row_list(compact)]
        for k, part in enumerate(choose(product, highs, count)):
            base = number * STEP + k
            nodes_ref[base] = part + own_ref[base].astype(jnp.float32)

    sweep(map_ref.shape[0] // STEP, body)
    kernel_copy.wait()
    square_ref[:npe, :npe] = kernel_ref[...]
    scale_copy.wait()
    scale = scale_ref[...]
    for state in range(0, count, 2):
        columns = jnp.concatenate(
            [nodes_ref[:, state, :], nodes_ref[:, state + 1, :]], axis=1
        ).astype(jnp.bfloat16)
        product = jnp.dot(square_ref[...], columns, preferred_element_type=jnp.float32)
        product_ref[:, state, :] = product[:, :128] * scale
        product_ref[:, state + 1, :] = product[:, 128:] * scale
    return rest


def scatter(map_ref, product_ref, total_ref, count):
    groups = total_ref.shape[0] // count
    zero = jnp.zeros((count, 128), jnp.bfloat16)
    total_ref[...] = jnp.zeros(total_ref.shape, jnp.float32)

    def body(number):
        block = block_of(map_ref, number)
        parts = []
        for k, row in enumerate(row_list(block)):
            high = high_part(row, LO).astype(jnp.float32).astype(jnp.bfloat16)
            high = jnp.broadcast_to(high, zero.shape)
            value = product_ref[number * STEP + k].astype(jnp.bfloat16)
            parts.append(
                jnp.concatenate(
                    [
                        jnp.where(high == jnp.full(zero.shape, group, jnp.bfloat16), value, zero)
                        for group in range(groups)
                    ],
                    axis=0,
                )
            )
        total_ref[...] += lax.dot_general(
            jnp.concatenate(parts, axis=1), marks_of(block, LO), (((1,), (1,)), ((), ())),
            preferred_element_type=jnp.float32,
        )

    sweep(map_ref.shape[0] // STEP, body)


def first_kernel(
    nbr_hbm, own_hbm, recv_hbm, map_hbm, kernel_hbm, scale_hbm, field_hbm, pot_hbm, send_hbm,
    next_hbm, out_hbm,
    own_ref, recv_ref, map_ref, kernel_ref, scale_ref,
    ghost_ref, square_ref, nodes_ref, product_ref,
    field_ref, pot_ref, send_ref, next_ref, table_ref, total_ref, out_ref,
    nbr_ref, sems,
):
    copies = Copies(sems)
    count, nodes = field_ref.shape

    def later():
        return [
            copies.start(field_hbm, field_ref),
            copies.start(pot_hbm, pot_ref),
            copies.start(send_hbm, send_ref),
        ]

    others = contract(
        copies, nbr_hbm, own_hbm, recv_hbm, map_hbm, kernel_hbm, scale_hbm,
        own_ref, recv_ref, map_ref, kernel_ref, scale_ref,
        ghost_ref, square_ref, nodes_ref, product_ref, nbr_ref, nodes, later,
    )
    scatter(map_ref, product_ref, total_ref, count)
    for copy in others:
        copy.wait()
    for group in range(field_ref.shape[1] // LO):
        lanes = slice(group * LO, (group + 1) * LO)
        rows = slice(group * count, (group + 1) * count)
        start = field_ref[:, lanes].astype(jnp.float32)
        image = total_ref[rows, :] + pot_ref[:, lanes] * start
        field = ((image - center * start) / half_width).astype(jnp.bfloat16)
        next_ref[:, lanes] = field
        table_ref[rows, :] = field
    next_copy = copies.start(next_ref, next_hbm)
    pack_sends(table_ref, send_ref, nbr_ref, out_ref, count)
    copies.start(out_ref, out_hbm).wait()
    next_copy.wait()


def energy_kernel(
    nbr_hbm, own_hbm, recv_hbm, map_hbm, kernel_hbm, scale_hbm, field_hbm, pot_hbm,
    cells_hbm, energy_ref,
    own_ref, recv_ref, map_ref, kernel_ref, scale_ref,
    ghost_ref, square_ref, nodes_ref, product_ref, field_ref, pot_ref, cells_ref, nbr_ref, sems,
):
    copies = Copies(sems)
    count, nodes = field_ref.shape

    def later():
        return [copies.start(field_hbm, field_ref), copies.start(pot_hbm, pot_ref)]

    others = contract(
        copies, nbr_hbm, own_hbm, recv_hbm, map_hbm, kernel_hbm, scale_hbm,
        own_ref, recv_ref, map_ref, kernel_ref, scale_ref,
        ghost_ref, square_ref, nodes_ref, product_ref, nbr_ref, nodes, later,
    )
    total = jnp.zeros((count, 128), jnp.float32)
    for base in range(own_ref.shape[0]):
        value = product_ref[base]
        cells_ref[base] = value.astype(jnp.bfloat16)
        total = total + value * own_ref[base].astype(jnp.float32)
    cells_copy = copies.start(cells_ref, cells_hbm)
    for copy in others:
        copy.wait()
    for base in range(0, nodes, 128):
        one = field_ref[:, base : base + 128].astype(jnp.float32)
        total = total + pot_ref[:, base : base + 128] * one * one
    sums = jnp.broadcast_to(jnp.sum(total, axis=1, keepdims=True), total.shape)
    state = lax.broadcasted_iota(jnp.int32, total.shape, 0)
    lane = lax.broadcasted_iota(jnp.int32, total.shape, 1)
    line = jnp.sum(jnp.where(state == lane, sums, 0.0), axis=0, keepdims=True)
    energy_ref[...] = jnp.broadcast_to(line[None], energy_ref.shape)
    cells_copy.wait()


def second_kernel(
    field_hbm, cells_hbm, map_hbm, pot_hbm, start_hbm, next_hbm, out_hbm,
    field_ref, cells_ref, map_ref, pot_ref, start_ref, next_ref, total_ref, sems,
):
    copies = Copies(sems)
    count = field_ref.shape[0]
    map_copy = read_map(copies, map_hbm, map_ref)
    cell_copy = copies.start(cells_hbm, cells_ref)
    others = [
        copies.start(field_hbm, field_ref),
        copies.start(pot_hbm, pot_ref),
        copies.start(start_hbm, start_ref),
    ]
    map_copy.wait()
    fill_map(map_ref, map_hbm.shape[0])
    cell_copy.wait()
    scatter(map_ref, cells_ref, total_ref, count)
    for copy in others:
        copy.wait()
    for group in range(field_ref.shape[1] // LO):
        lanes = slice(group * LO, (group + 1) * LO)
        rows = slice(group * count, (group + 1) * count)
        one = field_ref[:, lanes].astype(jnp.float32)
        start = start_ref[:, lanes].astype(jnp.float32)
        image = total_ref[rows, :] + pot_ref[:, lanes] * one
        next_ref[:, lanes] = (
            2.0 * (image - center * one) / half_width - start
        ).astype(jnp.bfloat16)
    width = out_hbm.shape[2]
    pending = [copies.start(next_ref, next_hbm)]
    for band in range(out_hbm.shape[0]):
        pending.append(
            copies.start(next_ref.at[:, band * width : (band + 1) * width], out_hbm.at[band])
        )
    for copy in pending:
        copy.wait()


def rotate_kernel(
    owner_hbm, rows_hbm, states_hbm, out_hbm, rows_ref, states_ref, out_ref, owner_ref, sems
):
    copies = Copies(sems)
    owner_copy = copies.start(owner_hbm, owner_ref)
    rows_copy = copies.start(rows_hbm, rows_ref)
    owner_copy.wait()
    count = states_hbm.shape[1]
    pending = [
        copies.start(states_hbm.at[owner_ref[k]], states_ref.at[pl.ds(k * count, count)])
        for k in range(owner_ref.shape[0])
    ]
    rows_copy.wait()
    for copy in pending:
        copy.wait()
    out_ref[...] = lax.dot_general(
        rows_ref[...], states_ref[...], (((0,), (0,)), ((), ())),
        preferred_element_type=jnp.float32,
    ).astype(jnp.bfloat16)
    copies.start(out_ref, out_hbm).wait()


vmem = pl.BlockSpec(memory_space=pltpu.VMEM)
hbm = pl.BlockSpec(memory_space=pltpu.HBM)
anywhere = pl.BlockSpec(memory_space=pl.ANY)
half = jnp.bfloat16
full = jnp.float32
whole = jnp.int32


def call(kernel, name, outs, scratch, scalars, sems, *operands, free=-1):
    held = [
        value if k == free else pltpu.with_memory_space_constraint(value, pltpu.HBM)
        for k, value in enumerate(operands)
    ]
    return pl.pallas_call(
        kernel,
        out_shape=tuple(
            jax.ShapeDtypeStruct(dims, kind) if place is vmem else pltpu.HBM(dims, kind)
            for dims, kind, place in outs
        ),
        in_specs=[anywhere if k == free else hbm for k in range(len(operands))],
        out_specs=tuple(place for _, _, place in outs),
        scratch_shapes=[pltpu.VMEM(dims, kind) for dims, kind in scratch]
        + [pltpu.SMEM(dims, jnp.int32) for dims in scalars]
        + [pltpu.SemaphoreType.DMA((sems,))],
        compiler_params=pltpu.CompilerParams(vmem_limit_bytes=48 << 20),
        name=name,
    )(*held)


def swap(value, axis):
    return lax.all_to_all(value, axis, split_axis=0, concat_axis=0, tiled=True)


def per_device(
    filter_block,
    local_pot,
    cell_scale,
    cell_kernel,
    cell_map,
    neighbour_ids,
    send_nodes,
    rotation_rows,
    panel_owner,
):
    count, nodes = filter_block.shape
    npe, cells = cell_map.shape
    mesh_size = lax.axis_size("mesh")
    band_size = lax.axis_size("band")
    width = nodes // band_size
    sends = send_nodes.transpose(1, 0, 2)
    pot = local_pot.reshape(1, -1)
    scale = cell_scale.reshape(1, -1)
    steps = -(-npe // (STEP * UNROLL)) * UNROLL
    padded = steps * STEP

    field_type = ((count, nodes), half)
    map_type = ((padded, cells), whole)
    send_type = (sends.shape, whole)
    pot_type = (pot.shape, full)
    table = ((nodes // LO * count, LO), half)
    total = ((nodes // LO * count, LO), full)
    outbox = ((mesh_size, count // 2, 128), half)
    columns = ((padded, count, cells), half)
    rows_type = (rotation_rows.shape, half)
    nbr_type = neighbour_ids.shape
    inner = [
        columns, outbox, map_type, (cell_kernel.shape, half), (scale.shape, full),
        ((send_nodes.size // GLO * count, GLO), half),
        ((padded, padded), half),
        ((padded, count, cells), full),
        ((padded, count, cells), full),
    ]

    panel_type = ((panel_owner.size * count, rotation_rows.shape[1]), half)
    outgoing, panels = call(
        pack_kernel, "pack", [outbox + (hbm,), ((band_size,) + panel_type[0], half, hbm)],
        [field_type, send_type, table, rows_type, panel_type, outbox],
        [nbr_type, panel_owner.shape], 6 + band_size,
        neighbour_ids, panel_owner, filter_block, sends, rotation_rows,
    )
    coefficients = lax.psum_scatter(panels, "band", scatter_dimension=0, tiled=True)[0]
    incoming = swap(outgoing, "mesh")
    def gather(field):
        return call(
            gather_kernel, "gather", [columns + (hbm,)],
            [field_type, map_type, columns, table], [], 3, field, cell_map,
        )

    (own,) = gather(filter_block)
    field_one, outgoing = call(
        first_kernel, "first", [field_type + (hbm,), outbox + (hbm,)],
        inner + [field_type, pot_type, send_type, field_type, table, total, outbox],
        [nbr_type], 11, neighbour_ids, own, incoming, cell_map, cell_kernel, scale,
        filter_block, pot, sends, free=2,
    )
    incoming = swap(outgoing, "mesh")
    (own,) = gather(field_one)
    products, energy = call(
        energy_kernel, "energy", [columns + (hbm,), ((mesh_size, 1, 128), full, vmem)],
        inner + [field_type, pot_type, columns], [nbr_type], 9,
        neighbour_ids, own, incoming, cell_map, cell_kernel, scale, field_one, pot, free=2,
    )
    energies = swap(energy, "mesh")
    filtered, parts = call(
        second_kernel, "second",
        [field_type + (hbm,), ((band_size, count, width), half, hbm)],
        [field_type, columns, map_type, pot_type, field_type, field_type, total],
        [], 6 + band_size, field_one, products, cell_map, pot, filter_block,
    )
    parts, energies = lax.optimization_barrier((parts, energies))
    states = swap(parts, "band")
    state_energy = jnp.sum(energies[:, 0, :count], axis=0) / (nodes * mesh_size)
    rotated_type = ((rotation_rows.shape[1], width), half)
    (rotated,) = call(
        rotate_kernel, "rotate", [rotated_type + (hbm,)],
        [
            panel_type,
            ((panel_owner.size * count, width), half),
            rotated_type,
        ],
        [panel_owner.shape], 3 + panel_owner.size, panel_owner, coefficients, states, free=2,
    )
    return (filtered, rotated, state_energy)


def solution(mesh):
    placed = (
        P("band", "mesh"),
        P("mesh"),
        P("mesh"),
        P(),
        P(None, "mesh"),
        P("mesh", None),
        P("mesh", None, None),
        P("band", None),
        P(),
    )
    return jax.shard_map(
        per_device,
        mesh=mesh,
        in_specs=placed,
        out_specs=(P("band", "mesh"), P(None, ("mesh", "band")), P("band")),
        check_vma=False,
    )
```

```python
import jax
import jax.numpy as jnp
from jax import lax
from jax.experimental import pallas as pl
from jax.experimental.pallas import tpu as pltpu
from jax.sharding import PartitionSpec as P

center = 6.0
half_width = 4.0
LO = 512
GLO = 128
STEP = 8
UNROLL = 16
SHORT = 8


def sweep(steps, body, unroll):
    def group(number, carry):
        for place in range(unroll):
            body(number * unroll + place)
        return carry

    lax.fori_loop(0, steps // unroll, group, 0)


def flags(row, width):
    parts = []
    level = lax.broadcasted_iota(jnp.int32, (min(width, 256), 128), 0)
    level = level.astype(jnp.float32).astype(jnp.bfloat16)
    one = jnp.ones(level.shape, jnp.bfloat16)
    zero = jnp.zeros(level.shape, jnp.bfloat16)
    for base in range(0, width, level.shape[0]):
        local = row - base
        local = jnp.where((local >= 0) & (local < level.shape[0]), local, -1)
        local = local.astype(jnp.float32).astype(jnp.bfloat16)
        parts.append(jnp.where(level == jnp.broadcast_to(local, level.shape), one, zero))
    return parts[0] if len(parts) == 1 else jnp.concatenate(parts, axis=0)


def low_part(row, width):
    return jnp.bitwise_and(row, width - 1)


def high_part(row, width):
    return jnp.right_shift(row, width.bit_length() - 1)


def choose(product, highs, count):
    groups = product.shape[0] // count
    picked = []
    for k, high in enumerate(highs):
        total = jnp.zeros((count, 128), jnp.float32)
        for group in range(groups):
            part = product[group * count : (group + 1) * count, k * 128 : (k + 1) * 128]
            total = jnp.where(high == group, part, total)
        picked.append(total)
    return picked


def row_list(block):
    return [block[k : k + 1, :] for k in range(block.shape[0])]


def stack_groups(field_ref, table_ref, count):
    for group in range(field_ref.shape[1] // LO):
        table_ref[group * count : (group + 1) * count, :] = field_ref[
            :, group * LO : (group + 1) * LO
        ]


class Copies:
    def __init__(self, sems):
        self.sems = sems
        self.used = 0

    def start(self, source, target):
        copy = pltpu.make_async_copy(source, target, self.sems.at[self.used])
        copy.start()
        self.used += 1
        return copy


def marks_of(block, width):
    return jnp.concatenate([flags(low_part(row, width), width) for row in row_list(block)], axis=1)


def read_map(copies, map_hbm, map_ref):
    npe = map_hbm.shape[0]
    return copies.start(map_hbm, map_ref.at[:npe])


def fill_map(map_ref, npe):
    rest = map_ref.shape[0] - npe
    map_ref[npe:, :] = jnp.full((rest, map_ref.shape[1]), -1, jnp.int32)


def block_of(ref, number):
    return ref[pl.ds(pl.multiple_of(number * STEP, STEP), STEP), :]


def pack_sends(table_ref, send_ref, nbr_ref, out_ref, count):
    out_ref[...] = jnp.zeros(out_ref.shape, out_ref.dtype)
    rows = [
        jnp.concatenate([send_ref[k], send_ref[k + 1]], axis=1)
        for k in range(0, send_ref.shape[0], 2)
    ]
    marks = jnp.concatenate([flags(low_part(row, LO), LO) for row in rows], axis=1)
    product = jnp.dot(table_ref[...], marks, preferred_element_type=jnp.float32)
    picked = choose(product, [high_part(row, LO) for row in rows], count)
    half = count // 2
    for k, part in enumerate(picked):
        for side in range(2):
            block = part[:, side * 64 : (side + 1) * 64]
            tile = jnp.concatenate([block[:half], block[half:]], axis=1)
            out_ref[nbr_ref[0, 2 * k + side]] = tile.astype(jnp.bfloat16)


def pack_kernel(
    nbr_hbm, field_hbm, send_hbm, out_hbm, field_ref, send_ref, table_ref, out_ref, nbr_ref, sems
):
    copies = Copies(sems)
    nbr_copy = copies.start(nbr_hbm, nbr_ref)
    field_copy = copies.start(field_hbm, field_ref)
    send_copy = copies.start(send_hbm, send_ref)
    count = field_ref.shape[0]
    field_copy.wait()
    stack_groups(field_ref, table_ref, count)
    send_copy.wait()
    nbr_copy.wait()
    pack_sends(table_ref, send_ref, nbr_ref, out_ref, count)
    copies.start(out_ref, out_hbm).wait()


def gather_chunk(table, block, marks, own_ref, number, count):
    product = jnp.dot(table, marks, preferred_element_type=jnp.float32)
    highs = [high_part(row, LO) for row in row_list(block)]
    for k, part in enumerate(choose(product, highs, count)):
        own_ref[number * STEP + k] = part.astype(jnp.bfloat16)


def gather_kernel(field_hbm, map_hbm, rows_hbm, own_hbm, copies_hbm, field_ref, map_ref, rows_ref, own_ref, table_ref, sems):
    copies = Copies(sems)
    field_copy = copies.start(field_hbm, field_ref)
    map_copy = read_map(copies, map_hbm, map_ref)
    rows_copy = copies.start(rows_hbm, rows_ref)
    count = field_ref.shape[0]
    field_copy.wait()
    stack_groups(field_ref, table_ref, count)
    rows_copy.wait()
    pending = [copies.start(rows_ref, copies_hbm.at[k]) for k in range(copies_hbm.shape[0])]
    map_copy.wait()
    fill_map(map_ref, map_hbm.shape[0])

    def body(number):
        block = block_of(map_ref, number)
        gather_chunk(table_ref[...], block, marks_of(block, LO), own_ref, number, count)

    sweep(map_ref.shape[0] // STEP, body, SHORT)
    copies.start(own_ref, own_hbm).wait()
    for copy in pending:
        copy.wait()


def contract(
    copies, nbr_hbm, own_hbm, recv_hbm, map_hbm, kernel_hbm, scale_hbm,
    own_ref, recv_ref, map_ref, kernel_ref, scale_ref,
    ghost_ref, square_ref, nodes_ref, product_ref, nbr_ref, nodes, later,
):
    count = own_ref.shape[1]
    npe = kernel_hbm.shape[0]
    half = count // 2
    nbr_copy = copies.start(nbr_hbm, nbr_ref)
    recv_copy = copies.start(recv_hbm, recv_ref)
    map_copy = read_map(copies, map_hbm, map_ref)
    own_copy = copies.start(own_hbm, own_ref)
    kernel_copy = copies.start(kernel_hbm, kernel_ref)
    scale_copy = copies.start(scale_hbm, scale_ref)
    rest = later()
    square_ref[...] = jnp.zeros(square_ref.shape, square_ref.dtype)
    nbr_copy.wait()
    neighbours = [nbr_ref[0, position] for position in range(nbr_ref.shape[1])]
    recv_copy.wait()
    for k in range(ghost_ref.shape[0] // count):
        left = recv_ref[neighbours[2 * k]]
        right = recv_ref[neighbours[2 * k + 1]]
        ghost_ref[k * count : k * count + half, :] = jnp.concatenate(
            [left[:, :64], right[:, :64]], axis=1
        )
        ghost_ref[k * count + half : (k + 1) * count, :] = jnp.concatenate(
            [left[:, 64:], right[:, 64:]], axis=1
        )
    map_copy.wait()
    fill_map(map_ref, map_hbm.shape[0])
    own_copy.wait()

    def body(number):
        slot = block_of(map_ref, number) - nodes
        owner = jnp.right_shift(slot, 6)
        place = jnp.full(slot.shape, -1, jnp.int32)
        for position, neighbour in enumerate(neighbours):
            place = jnp.where(owner == neighbour, position, place)
        compact = jnp.where(place >= 0, place * 64 + jnp.bitwise_and(slot, 63), -1)
        product = jnp.dot(
            ghost_ref[...], marks_of(compact, GLO), preferred_element_type=jnp.float32
        )
        highs = [high_part(row, GLO) for row in row_list(compact)]
        for k, part in enumerate(choose(product, highs, count)):
            base = number * STEP + k
            nodes_ref[base] = part + own_ref[base].astype(jnp.float32)

    sweep(map_ref.shape[0] // STEP, body, UNROLL)
    kernel_copy.wait()
    square_ref[:npe, :npe] = kernel_ref[...]
    scale_copy.wait()
    scale = scale_ref[...]
    for state in range(0, count, 2):
        columns = jnp.concatenate(
            [nodes_ref[:, state, :], nodes_ref[:, state + 1, :]], axis=1
        ).astype(jnp.bfloat16)
        product = jnp.dot(square_ref[...], columns, preferred_element_type=jnp.float32)
        product_ref[:, state, :] = product[:, :128] * scale
        product_ref[:, state + 1, :] = product[:, 128:] * scale
    return rest


def scatter(map_ref, product_ref, total_ref, count):
    groups = total_ref.shape[0] // count
    zero = jnp.zeros((count, 128), jnp.bfloat16)
    total_ref[...] = jnp.zeros(total_ref.shape, jnp.float32)

    def body(number):
        block = block_of(map_ref, number)
        parts = []
        for k, row in enumerate(row_list(block)):
            high = high_part(row, LO).astype(jnp.float32).astype(jnp.bfloat16)
            high = jnp.broadcast_to(high, zero.shape)
            value = product_ref[number * STEP + k].astype(jnp.bfloat16)
            parts.append(
                jnp.concatenate(
                    [
                        jnp.where(high == jnp.full(zero.shape, group, jnp.bfloat16), value, zero)
                        for group in range(groups)
                    ],
                    axis=0,
                )
            )
        total_ref[...] += lax.dot_general(
            jnp.concatenate(parts, axis=1), marks_of(block, LO), (((1,), (1,)), ((), ())),
            preferred_element_type=jnp.float32,
        )

    sweep(map_ref.shape[0] // STEP, body, UNROLL)


def first_kernel(
    nbr_hbm, own_hbm, recv_hbm, map_hbm, kernel_hbm, scale_hbm, field_hbm, pot_hbm, send_hbm,
    next_hbm, out_hbm,
    own_ref, recv_ref, map_ref, kernel_ref, scale_ref,
    ghost_ref, square_ref, nodes_ref, product_ref,
    field_ref, pot_ref, send_ref, next_ref, table_ref, total_ref, out_ref,
    nbr_ref, sems,
):
    copies = Copies(sems)
    count, nodes = field_ref.shape

    def later():
        return [
            copies.start(field_hbm, field_ref),
            copies.start(pot_hbm, pot_ref),
            copies.start(send_hbm, send_ref),
        ]

    others = contract(
        copies, nbr_hbm, own_hbm, recv_hbm, map_hbm, kernel_hbm, scale_hbm,
        own_ref, recv_ref, map_ref, kernel_ref, scale_ref,
        ghost_ref, square_ref, nodes_ref, product_ref, nbr_ref, nodes, later,
    )
    scatter(map_ref, product_ref, total_ref, count)
    for copy in others:
        copy.wait()
    for group in range(field_ref.shape[1] // LO):
        lanes = slice(group * LO, (group + 1) * LO)
        rows = slice(group * count, (group + 1) * count)
        start = field_ref[:, lanes].astype(jnp.float32)
        image = total_ref[rows, :] + pot_ref[:, lanes] * start
        field = ((image - center * start) / half_width).astype(jnp.bfloat16)
        next_ref[:, lanes] = field
        table_ref[rows, :] = field
    next_copy = copies.start(next_ref, next_hbm)
    pack_sends(table_ref, send_ref, nbr_ref, out_ref, count)
    copies.start(out_ref, out_hbm).wait()
    next_copy.wait()


def energy_kernel(
    nbr_hbm, own_hbm, recv_hbm, map_hbm, kernel_hbm, scale_hbm, field_hbm, pot_hbm,
    cells_hbm, energy_ref,
    own_ref, recv_ref, map_ref, kernel_ref, scale_ref,
    ghost_ref, square_ref, nodes_ref, product_ref, field_ref, pot_ref, cells_ref, nbr_ref, sems,
):
    copies = Copies(sems)
    count, nodes = field_ref.shape

    def later():
        return [copies.start(field_hbm, field_ref), copies.start(pot_hbm, pot_ref)]

    others = contract(
        copies, nbr_hbm, own_hbm, recv_hbm, map_hbm, kernel_hbm, scale_hbm,
        own_ref, recv_ref, map_ref, kernel_ref, scale_ref,
        ghost_ref, square_ref, nodes_ref, product_ref, nbr_ref, nodes, later,
    )
    total = jnp.zeros((count, 128), jnp.float32)
    for base in range(own_ref.shape[0]):
        value = product_ref[base]
        cells_ref[base] = value.astype(jnp.bfloat16)
        total = total + value * own_ref[base].astype(jnp.float32)
    cells_copy = copies.start(cells_ref, cells_hbm)
    for copy in others:
        copy.wait()
    for base in range(0, nodes, 128):
        one = field_ref[:, base : base + 128].astype(jnp.float32)
        total = total + pot_ref[:, base : base + 128] * one * one
    sums = jnp.broadcast_to(jnp.sum(total, axis=1, keepdims=True), total.shape)
    state = lax.broadcasted_iota(jnp.int32, total.shape, 0)
    lane = lax.broadcasted_iota(jnp.int32, total.shape, 1)
    line = jnp.sum(jnp.where(state == lane, sums, 0.0), axis=0, keepdims=True)
    energy_ref[...] = jnp.broadcast_to(line[None], energy_ref.shape)
    cells_copy.wait()


def second_kernel(
    field_hbm, cells_hbm, map_hbm, pot_hbm, start_hbm, next_hbm, out_ref,
    field_ref, cells_ref, map_ref, pot_ref, start_ref, next_ref, total_ref, sems,
):
    copies = Copies(sems)
    count = field_ref.shape[0]
    map_copy = read_map(copies, map_hbm, map_ref)
    cell_copy = copies.start(cells_hbm, cells_ref)
    others = [
        copies.start(field_hbm, field_ref),
        copies.start(pot_hbm, pot_ref),
        copies.start(start_hbm, start_ref),
    ]
    map_copy.wait()
    fill_map(map_ref, map_hbm.shape[0])
    cell_copy.wait()
    scatter(map_ref, cells_ref, total_ref, count)
    for copy in others:
        copy.wait()
    for group in range(field_ref.shape[1] // LO):
        lanes = slice(group * LO, (group + 1) * LO)
        rows = slice(group * count, (group + 1) * count)
        one = field_ref[:, lanes].astype(jnp.float32)
        start = start_ref[:, lanes].astype(jnp.float32)
        image = total_ref[rows, :] + pot_ref[:, lanes] * one
        next_ref[:, lanes] = (
            2.0 * (image - center * one) / half_width - start
        ).astype(jnp.bfloat16)
    next_copy = copies.start(next_ref, next_hbm)
    width = out_ref.shape[2]
    for band in range(out_ref.shape[0]):
        out_ref[band] = next_ref[:, band * width : (band + 1) * width]
    next_copy.wait()


def rotate_kernel(
    owner_ref, rows_hbm, states_hbm, out_hbm, rows_ref, states_ref, out_ref, sems
):
    copies = Copies(sems)
    pending = []
    count = rows_hbm.shape[1]
    for k in range(owner_ref.shape[0]):
        place = pl.ds(k * count, count)
        pending.append(copies.start(rows_hbm.at[owner_ref[k]], rows_ref.at[place]))
        pending.append(copies.start(states_hbm.at[owner_ref[k]], states_ref.at[place]))
    for copy in pending:
        copy.wait()
    out_ref[...] = lax.dot_general(
        rows_ref[...], states_ref[...], (((0,), (0,)), ((), ())),
        preferred_element_type=jnp.float32,
    ).astype(jnp.bfloat16)
    copies.start(out_ref, out_hbm).wait()


vmem = pl.BlockSpec(memory_space=pltpu.VMEM)
hbm = pl.BlockSpec(memory_space=pltpu.HBM)
smem = pl.BlockSpec(memory_space=pltpu.SMEM)
anywhere = pl.BlockSpec(memory_space=pl.ANY)
half = jnp.bfloat16
full = jnp.float32
whole = jnp.int32


def call(kernel, name, outs, scratch, scalars, sems, *operands, free=-1, number=-1):
    held = [
        value if k in (free, number) else pltpu.with_memory_space_constraint(value, pltpu.HBM)
        for k, value in enumerate(operands)
    ]
    return pl.pallas_call(
        kernel,
        out_shape=tuple(
            jax.ShapeDtypeStruct(dims, kind) if place is vmem else pltpu.HBM(dims, kind)
            for dims, kind, place in outs
        ),
        in_specs=[
            anywhere if k == free else smem if k == number else hbm for k in range(len(operands))
        ],
        out_specs=tuple(place for _, _, place in outs),
        scratch_shapes=[pltpu.VMEM(dims, kind) for dims, kind in scratch]
        + [pltpu.SMEM(dims, jnp.int32) for dims in scalars]
        + [pltpu.SemaphoreType.DMA((sems,))],
        compiler_params=pltpu.CompilerParams(vmem_limit_bytes=48 << 20),
        name=name,
    )(*held)


def swap(value, axis):
    return lax.all_to_all(value, axis, split_axis=0, concat_axis=0, tiled=True)


def per_device(
    filter_block,
    local_pot,
    cell_scale,
    cell_kernel,
    cell_map,
    neighbour_ids,
    send_nodes,
    rotation_rows,
    panel_owner,
):
    count, nodes = filter_block.shape
    npe, cells = cell_map.shape
    mesh_size = lax.axis_size("mesh")
    band_size = lax.axis_size("band")
    width = nodes // band_size
    sends = send_nodes.transpose(1, 0, 2)
    pot = local_pot.reshape(1, -1)
    scale = cell_scale.reshape(1, -1)
    steps = -(-npe // (STEP * UNROLL)) * UNROLL
    padded = steps * STEP

    field_type = ((count, nodes), half)
    map_type = ((padded, cells), whole)
    send_type = (sends.shape, whole)
    pot_type = (pot.shape, full)
    table = ((nodes // LO * count, LO), half)
    total = ((nodes // LO * count, LO), full)
    outbox = ((mesh_size, count // 2, 128), half)
    columns = ((padded, count, cells), half)
    rows_type = (rotation_rows.shape, half)
    nbr_type = neighbour_ids.shape
    inner = [
        columns, outbox, map_type, (cell_kernel.shape, half), (scale.shape, full),
        ((send_nodes.size // GLO * count, GLO), half),
        ((padded, padded), half),
        ((padded, count, cells), full),
        ((padded, count, cells), full),
    ]

    (outgoing,) = call(
        pack_kernel, "pack", [outbox + (hbm,)], [field_type, send_type, table, outbox],
        [nbr_type], 4, neighbour_ids, filter_block, sends,
    )
    incoming = swap(outgoing, "mesh")
    copies_type = ((band_size,) + rotation_rows.shape, half)

    def gather(field):
        return call(
            gather_kernel, "gather", [columns + (hbm,), copies_type + (hbm,)],
            [field_type, map_type, rows_type, columns, table], [], 4 + band_size,
            field, cell_map, rotation_rows,
        )

    own, row_copies = gather(filter_block)
    field_one, outgoing = call(
        first_kernel, "first", [field_type + (hbm,), outbox + (hbm,)],
        inner + [field_type, pot_type, send_type, field_type, table, total, outbox],
        [nbr_type], 11, neighbour_ids, own, incoming, cell_map, cell_kernel, scale,
        filter_block, pot, sends, free=2,
    )
    all_rows = swap(row_copies, "band")
    outgoing, all_rows = lax.optimization_barrier((outgoing, all_rows))
    incoming = swap(outgoing, "mesh")
    own, _ = gather(field_one)
    products, energy = call(
        energy_kernel, "energy", [columns + (hbm,), ((mesh_size, 1, 128), full, vmem)],
        inner + [field_type, pot_type, columns], [nbr_type], 9,
        neighbour_ids, own, incoming, cell_map, cell_kernel, scale, field_one, pot, free=2,
    )
    energies = swap(energy, "mesh")
    filtered, parts = call(
        second_kernel, "second",
        [field_type + (hbm,), ((band_size, count, width), half, vmem)],
        [field_type, columns, map_type, pot_type, field_type, field_type, total],
        [], 6, field_one, products, cell_map, pot, filter_block,
    )
    state_energy = jnp.sum(energies[:, 0, :count], axis=0) / (nodes * mesh_size)
    parts, state_energy = lax.optimization_barrier((parts, state_energy))
    states = swap(parts, "band")
    rotated_type = ((rotation_rows.shape[1], width), half)
    (rotated,) = call(
        rotate_kernel, "rotate", [rotated_type + (hbm,)],
        [
            ((panel_owner.size * count, rotation_rows.shape[1]), half),
            ((panel_owner.size * count, width), half),
            rotated_type,
        ],
        [], 1 + 2 * panel_owner.size, panel_owner, all_rows, states, free=2, number=0,
    )
    return (filtered, rotated, state_energy)


def solution(mesh):
    placed = (
        P("band", "mesh"),
        P("mesh"),
        P("mesh"),
        P(),
        P(None, "mesh"),
        P("mesh", None),
        P("mesh", None, None),
        P("band", None),
        P(),
    )
    return jax.shard_map(
        per_device,
        mesh=mesh,
        in_specs=placed,
        out_specs=(P("band", "mesh"), P(None, ("mesh", "band")), P("band")),
        check_vma=False,
    )
```

```python
import jax
import jax.numpy as jnp
from jax import lax
from jax.experimental import pallas as pl
from jax.experimental.pallas import tpu as pltpu
from jax.sharding import PartitionSpec as P

center = 6.0
half_width = 4.0
LO = 512
GLO = 128
STEP = 8
UNROLL = 16
SHORT = 8
PIECE = 32


def sweep(steps, body, unroll):
    def group(number, carry):
        for place in range(unroll):
            body(number * unroll + place)
        return carry

    if steps == unroll:
        group(0, 0)
    else:
        lax.fori_loop(0, steps // unroll, group, 0)


def flags(row, width):
    parts = []
    level = lax.broadcasted_iota(jnp.int32, (min(width, 256), 128), 0)
    level = level.astype(jnp.float32).astype(jnp.bfloat16)
    one = jnp.ones(level.shape, jnp.bfloat16)
    zero = jnp.zeros(level.shape, jnp.bfloat16)
    for base in range(0, width, level.shape[0]):
        local = row - base
        local = jnp.where((local >= 0) & (local < level.shape[0]), local, -1)
        local = local.astype(jnp.float32).astype(jnp.bfloat16)
        parts.append(jnp.where(level == jnp.broadcast_to(local, level.shape), one, zero))
    return parts[0] if len(parts) == 1 else jnp.concatenate(parts, axis=0)


def low_part(row, width):
    return jnp.bitwise_and(row, width - 1)


def high_part(row, width):
    return jnp.right_shift(row, width.bit_length() - 1)


def choose(product, highs, count):
    groups = product.shape[0] // count
    picked = []
    for k, high in enumerate(highs):
        total = jnp.zeros((count, 128), jnp.float32)
        for group in range(groups):
            part = product[group * count : (group + 1) * count, k * 128 : (k + 1) * 128]
            total = jnp.where(high == group, part, total)
        picked.append(total)
    return picked


def row_list(block):
    return [block[k : k + 1, :] for k in range(block.shape[0])]


def stack_groups(field_ref, table_ref, count):
    for group in range(field_ref.shape[1] // LO):
        table_ref[group * count : (group + 1) * count, :] = field_ref[
            :, group * LO : (group + 1) * LO
        ]


class Copies:
    def __init__(self, sems):
        self.sems = sems
        self.used = 0

    def start(self, source, target):
        copy = pltpu.make_async_copy(source, target, self.sems.at[self.used])
        copy.start()
        self.used += 1
        return copy


def marks_of(block, width):
    return jnp.concatenate([flags(low_part(row, width), width) for row in row_list(block)], axis=1)


def read_map(copies, map_hbm, map_ref):
    npe = map_hbm.shape[0]
    return copies.start(map_hbm, map_ref.at[:npe])


def fill_map(map_ref, npe):
    rest = map_ref.shape[0] - npe
    map_ref[npe:, :] = jnp.full((rest, map_ref.shape[1]), -1, jnp.int32)


def block_of(ref, number):
    base = number * STEP
    if not isinstance(base, int):
        base = pl.multiple_of(base, STEP)
    return ref[pl.ds(base, STEP), :]


def pack_sends(table_ref, send_ref, nbr_ref, out_ref, count):
    out_ref[...] = jnp.zeros(out_ref.shape, out_ref.dtype)
    rows = [
        jnp.concatenate([send_ref[k], send_ref[k + 1]], axis=1)
        for k in range(0, send_ref.shape[0], 2)
    ]
    marks = jnp.concatenate([flags(low_part(row, LO), LO) for row in rows], axis=1)
    product = jnp.dot(table_ref[...], marks, preferred_element_type=jnp.float32)
    picked = choose(product, [high_part(row, LO) for row in rows], count)
    half = count // 2
    for k, part in enumerate(picked):
        for side in range(2):
            block = part[:, side * 64 : (side + 1) * 64]
            tile = jnp.concatenate([block[:half], block[half:]], axis=1)
            out_ref[nbr_ref[0, 2 * k + side]] = tile.astype(jnp.bfloat16)


def pack_kernel(
    nbr_hbm, field_hbm, send_hbm, out_hbm, field_ref, send_ref, table_ref, out_ref, nbr_ref, sems
):
    copies = Copies(sems)
    nbr_copy = copies.start(nbr_hbm, nbr_ref)
    field_copy = copies.start(field_hbm, field_ref)
    send_copy = copies.start(send_hbm, send_ref)
    count = field_ref.shape[0]
    field_copy.wait()
    stack_groups(field_ref, table_ref, count)
    send_copy.wait()
    nbr_copy.wait()
    pack_sends(table_ref, send_ref, nbr_ref, out_ref, count)
    copies.start(out_ref, out_hbm).wait()


def gather_chunk(table, block, marks, own_ref, number, count):
    product = jnp.dot(table, marks, preferred_element_type=jnp.float32)
    highs = [high_part(row, LO) for row in row_list(block)]
    for k, part in enumerate(choose(product, highs, count)):
        own_ref[number * STEP + k] = part.astype(jnp.bfloat16)


def gather_kernel(field_hbm, map_hbm, rows_hbm, own_hbm, copies_hbm, field_ref, map_ref, rows_ref, own_ref, table_ref, sems):
    copies = Copies(sems)
    field_copy = copies.start(field_hbm, field_ref)
    map_copy = read_map(copies, map_hbm, map_ref)
    rows_copy = copies.start(rows_hbm, rows_ref)
    count = field_ref.shape[0]
    field_copy.wait()
    stack_groups(field_ref, table_ref, count)
    rows_copy.wait()
    pending = [copies.start(rows_ref, copies_hbm.at[k]) for k in range(copies_hbm.shape[0])]
    map_copy.wait()
    fill_map(map_ref, map_hbm.shape[0])

    def body(number):
        block = block_of(map_ref, number)
        gather_chunk(table_ref[...], block, marks_of(block, LO), own_ref, number, count)

    sweep(map_ref.shape[0] // STEP, body, SHORT)
    copies.start(own_ref, own_hbm).wait()
    for copy in pending:
        copy.wait()


def contract(
    copies, nbr_hbm, own_hbm, recv_hbm, map_hbm, kernel_hbm, scale_hbm,
    own_ref, recv_ref, map_ref, kernel_ref, scale_ref,
    ghost_ref, square_ref, nodes_ref, product_ref, nbr_ref, nodes, later,
):
    count = own_ref.shape[1]
    npe = kernel_hbm.shape[0]
    half = count // 2
    nbr_copy = copies.start(nbr_hbm, nbr_ref)
    recv_copy = copies.start(recv_hbm, recv_ref)
    map_copy = read_map(copies, map_hbm, map_ref)
    own_copy = copies.start(own_hbm, own_ref)
    kernel_copy = copies.start(kernel_hbm, kernel_ref)
    scale_copy = copies.start(scale_hbm, scale_ref)
    rest = later()
    square_ref[...] = jnp.zeros(square_ref.shape, square_ref.dtype)
    nbr_copy.wait()
    neighbours = [nbr_ref[0, position] for position in range(nbr_ref.shape[1])]
    recv_copy.wait()
    for k in range(ghost_ref.shape[0] // count):
        left = recv_ref[neighbours[2 * k]]
        right = recv_ref[neighbours[2 * k + 1]]
        ghost_ref[k * count : k * count + half, :] = jnp.concatenate(
            [left[:, :64], right[:, :64]], axis=1
        )
        ghost_ref[k * count + half : (k + 1) * count, :] = jnp.concatenate(
            [left[:, 64:], right[:, 64:]], axis=1
        )
    map_copy.wait()
    fill_map(map_ref, map_hbm.shape[0])
    own_copy.wait()

    def body(number):
        slot = block_of(map_ref, number) - nodes
        owner = jnp.right_shift(slot, 6)
        place = jnp.full(slot.shape, -1, jnp.int32)
        for position, neighbour in enumerate(neighbours):
            place = jnp.where(owner == neighbour, position, place)
        compact = jnp.where(place >= 0, place * 64 + jnp.bitwise_and(slot, 63), -1)
        product = jnp.dot(
            ghost_ref[...], marks_of(compact, GLO), preferred_element_type=jnp.float32
        )
        highs = [high_part(row, GLO) for row in row_list(compact)]
        for k, part in enumerate(choose(product, highs, count)):
            base = number * STEP + k
            nodes_ref[base] = part + own_ref[base].astype(jnp.float32)

    sweep(map_ref.shape[0] // STEP, body, UNROLL)
    kernel_copy.wait()
    square_ref[:npe, :npe] = kernel_ref[...]
    scale_copy.wait()
    scale = scale_ref[...]
    for state in range(0, count, 2):
        columns = jnp.concatenate(
            [nodes_ref[:, state, :], nodes_ref[:, state + 1, :]], axis=1
        ).astype(jnp.bfloat16)
        product = jnp.dot(square_ref[...], columns, preferred_element_type=jnp.float32)
        product_ref[:, state, :] = product[:, :128] * scale
        product_ref[:, state + 1, :] = product[:, 128:] * scale
    return rest


def scatter(map_ref, product_ref, total_ref, count):
    groups = total_ref.shape[0] // count
    zero = jnp.zeros((count, 128), jnp.bfloat16)
    total_ref[...] = jnp.zeros(total_ref.shape, jnp.float32)

    def body(number):
        block = block_of(map_ref, number)
        parts = []
        for k, row in enumerate(row_list(block)):
            high = high_part(row, LO).astype(jnp.float32).astype(jnp.bfloat16)
            high = jnp.broadcast_to(high, zero.shape)
            value = product_ref[number * STEP + k].astype(jnp.bfloat16)
            parts.append(
                jnp.concatenate(
                    [
                        jnp.where(high == jnp.full(zero.shape, group, jnp.bfloat16), value, zero)
                        for group in range(groups)
                    ],
                    axis=0,
                )
            )
        total_ref[...] += lax.dot_general(
            jnp.concatenate(parts, axis=1), marks_of(block, LO), (((1,), (1,)), ((), ())),
            preferred_element_type=jnp.float32,
        )

    sweep(map_ref.shape[0] // STEP, body, UNROLL)


def first_kernel(
    nbr_hbm, own_hbm, recv_hbm, map_hbm, kernel_hbm, scale_hbm, field_hbm, pot_hbm, send_hbm,
    next_hbm, out_hbm,
    own_ref, recv_ref, map_ref, kernel_ref, scale_ref,
    ghost_ref, square_ref, nodes_ref, product_ref,
    field_ref, pot_ref, send_ref, next_ref, table_ref, total_ref, out_ref,
    nbr_ref, sems,
):
    copies = Copies(sems)
    count, nodes = field_ref.shape

    def later():
        return [
            copies.start(field_hbm, field_ref),
            copies.start(pot_hbm, pot_ref),
            copies.start(send_hbm, send_ref),
        ]

    others = contract(
        copies, nbr_hbm, own_hbm, recv_hbm, map_hbm, kernel_hbm, scale_hbm,
        own_ref, recv_ref, map_ref, kernel_ref, scale_ref,
        ghost_ref, square_ref, nodes_ref, product_ref, nbr_ref, nodes, later,
    )
    scatter(map_ref, product_ref, total_ref, count)
    for copy in others:
        copy.wait()
    for group in range(field_ref.shape[1] // LO):
        lanes = slice(group * LO, (group + 1) * LO)
        rows = slice(group * count, (group + 1) * count)
        start = field_ref[:, lanes].astype(jnp.float32)
        image = total_ref[rows, :] + pot_ref[:, lanes] * start
        field = ((image - center * start) / half_width).astype(jnp.bfloat16)
        next_ref[:, lanes] = field
        table_ref[rows, :] = field
    next_copy = copies.start(next_ref, next_hbm)
    pack_sends(table_ref, send_ref, nbr_ref, out_ref, count)
    copies.start(out_ref, out_hbm).wait()
    next_copy.wait()


def energy_kernel(
    nbr_hbm, own_hbm, recv_hbm, map_hbm, kernel_hbm, scale_hbm, field_hbm, pot_hbm,
    cells_hbm, energy_ref,
    own_ref, recv_ref, map_ref, kernel_ref, scale_ref,
    ghost_ref, square_ref, nodes_ref, product_ref, field_ref, pot_ref, cells_ref, nbr_ref, sems,
):
    copies = Copies(sems)
    count, nodes = field_ref.shape

    def later():
        return [copies.start(field_hbm, field_ref), copies.start(pot_hbm, pot_ref)]

    others = contract(
        copies, nbr_hbm, own_hbm, recv_hbm, map_hbm, kernel_hbm, scale_hbm,
        own_ref, recv_ref, map_ref, kernel_ref, scale_ref,
        ghost_ref, square_ref, nodes_ref, product_ref, nbr_ref, nodes, later,
    )
    total = jnp.zeros((count, 128), jnp.float32)
    pending = []
    for base in range(own_ref.shape[0]):
        value = product_ref[base]
        cells_ref[base] = value.astype(jnp.bfloat16)
        total = total + value * own_ref[base].astype(jnp.float32)
        if (base + 1) % PIECE == 0:
            piece = slice(base + 1 - PIECE, base + 1)
            pending.append(copies.start(cells_ref.at[piece], cells_hbm.at[piece]))
    for copy in others:
        copy.wait()
    for base in range(0, nodes, 128):
        one = field_ref[:, base : base + 128].astype(jnp.float32)
        total = total + pot_ref[:, base : base + 128] * one * one
    sums = jnp.broadcast_to(jnp.sum(total, axis=1, keepdims=True), total.shape)
    state = lax.broadcasted_iota(jnp.int32, total.shape, 0)
    lane = lax.broadcasted_iota(jnp.int32, total.shape, 1)
    line = jnp.sum(jnp.where(state == lane, sums, 0.0), axis=0, keepdims=True)
    energy_ref[...] = jnp.broadcast_to(line[None], energy_ref.shape)
    for copy in pending:
        copy.wait()


def second_kernel(
    field_hbm, cells_hbm, map_hbm, pot_hbm, start_hbm, next_hbm, out_ref,
    field_ref, cells_ref, map_ref, pot_ref, start_ref, next_ref, total_ref, sems,
):
    copies = Copies(sems)
    count = field_ref.shape[0]
    map_copy = read_map(copies, map_hbm, map_ref)
    cell_copy = copies.start(cells_hbm, cells_ref)
    others = [
        copies.start(field_hbm, field_ref),
        copies.start(pot_hbm, pot_ref),
        copies.start(start_hbm, start_ref),
    ]
    map_copy.wait()
    fill_map(map_ref, map_hbm.shape[0])
    cell_copy.wait()
    scatter(map_ref, cells_ref, total_ref, count)
    for copy in others:
        copy.wait()
    for group in range(field_ref.shape[1] // LO):
        lanes = slice(group * LO, (group + 1) * LO)
        rows = slice(group * count, (group + 1) * count)
        one = field_ref[:, lanes].astype(jnp.float32)
        start = start_ref[:, lanes].astype(jnp.float32)
        image = total_ref[rows, :] + pot_ref[:, lanes] * one
        next_ref[:, lanes] = (
            2.0 * (image - center * one) / half_width - start
        ).astype(jnp.bfloat16)
    next_copy = copies.start(next_ref, next_hbm)
    width = out_ref.shape[2]
    for band in range(out_ref.shape[0]):
        out_ref[band] = next_ref[:, band * width : (band + 1) * width]
    next_copy.wait()


def rotate_kernel(owner_ref, rows_ref, states_ref, out_hbm, out_ref, sems):
    copies = Copies(sems)
    owners = [owner_ref[k] for k in range(owner_ref.shape[0])]
    rows = jnp.concatenate([rows_ref[owner] for owner in owners], axis=0)
    panels = jnp.concatenate([states_ref[owner] for owner in owners], axis=0)
    size = out_ref.shape[0] // 2
    pending = []
    for side in range(2):
        piece = slice(side * size, (side + 1) * size)
        out_ref[piece, :] = lax.dot_general(
            rows[:, piece], panels, (((0,), (0,)), ((), ())), preferred_element_type=jnp.float32
        ).astype(jnp.bfloat16)
        pending.append(copies.start(out_ref.at[piece], out_hbm.at[piece]))
    for copy in pending:
        copy.wait()


vmem = pl.BlockSpec(memory_space=pltpu.VMEM)
hbm = pl.BlockSpec(memory_space=pltpu.HBM)
smem = pl.BlockSpec(memory_space=pltpu.SMEM)
anywhere = pl.BlockSpec(memory_space=pl.ANY)
half = jnp.bfloat16
full = jnp.float32
whole = jnp.int32


def call(kernel, name, outs, scratch, scalars, sems, *operands, free=-1, places=None):
    if places is None:
        places = [anywhere if k == free else hbm for k in range(len(operands))]
    held = [
        pltpu.with_memory_space_constraint(value, pltpu.HBM) if place is hbm else value
        for place, value in zip(places, operands)
    ]
    return pl.pallas_call(
        kernel,
        out_shape=tuple(
            jax.ShapeDtypeStruct(dims, kind) if place is vmem else pltpu.HBM(dims, kind)
            for dims, kind, place in outs
        ),
        in_specs=list(places),
        out_specs=tuple(place for _, _, place in outs),
        scratch_shapes=[pltpu.VMEM(dims, kind) for dims, kind in scratch]
        + [pltpu.SMEM(dims, jnp.int32) for dims in scalars]
        + [pltpu.SemaphoreType.DMA((sems,))],
        compiler_params=pltpu.CompilerParams(vmem_limit_bytes=48 << 20),
        name=name,
    )(*held)


def swap(value, axis):
    return lax.all_to_all(value, axis, split_axis=0, concat_axis=0, tiled=True)


def per_device(
    filter_block,
    local_pot,
    cell_scale,
    cell_kernel,
    cell_map,
    neighbour_ids,
    send_nodes,
    rotation_rows,
    panel_owner,
):
    count, nodes = filter_block.shape
    npe, cells = cell_map.shape
    mesh_size = lax.axis_size("mesh")
    band_size = lax.axis_size("band")
    width = nodes // band_size
    sends = send_nodes.transpose(1, 0, 2)
    pot = local_pot.reshape(1, -1)
    scale = cell_scale.reshape(1, -1)
    steps = -(-npe // (STEP * UNROLL)) * UNROLL
    padded = steps * STEP

    field_type = ((count, nodes), half)
    map_type = ((padded, cells), whole)
    send_type = (sends.shape, whole)
    pot_type = (pot.shape, full)
    table = ((nodes // LO * count, LO), half)
    total = ((nodes // LO * count, LO), full)
    outbox = ((mesh_size, count // 2, 128), half)
    columns = ((padded, count, cells), half)
    rows_type = (rotation_rows.shape, half)
    nbr_type = neighbour_ids.shape
    inner = [
        columns, outbox, map_type, (cell_kernel.shape, half), (scale.shape, full),
        ((send_nodes.size // GLO * count, GLO), half),
        ((padded, padded), half),
        ((padded, count, cells), full),
        ((padded, count, cells), full),
    ]

    (outgoing,) = call(
        pack_kernel, "pack", [outbox + (hbm,)], [field_type, send_type, table, outbox],
        [nbr_type], 4, neighbour_ids, filter_block, sends,
    )
    incoming = swap(outgoing, "mesh")
    copies_type = ((band_size,) + rotation_rows.shape, half)

    def gather(field):
        return call(
            gather_kernel, "gather", [columns + (hbm,), copies_type + (hbm,)],
            [field_type, map_type, rows_type, columns, table], [], 4 + band_size,
            field, cell_map, rotation_rows,
        )

    own, row_copies = gather(filter_block)
    field_one, outgoing = call(
        first_kernel, "first", [field_type + (hbm,), outbox + (hbm,)],
        inner + [field_type, pot_type, send_type, field_type, table, total, outbox],
        [nbr_type], 11, neighbour_ids, own, incoming, cell_map, cell_kernel, scale,
        filter_block, pot, sends, free=2,
    )
    all_rows = swap(row_copies, "band")
    outgoing, all_rows = lax.optimization_barrier((outgoing, all_rows))
    incoming = swap(outgoing, "mesh")
    own, _ = gather(field_one)
    products, energy = call(
        energy_kernel, "energy", [columns + (hbm,), ((mesh_size, 1, 128), full, vmem)],
        inner + [field_type, pot_type, columns], [nbr_type], 8 + padded // PIECE,
        neighbour_ids, own, incoming, cell_map, cell_kernel, scale, field_one, pot, free=2,
    )
    energies = swap(energy, "mesh")
    filtered, parts = call(
        second_kernel, "second",
        [field_type + (hbm,), ((band_size, count, width), half, vmem)],
        [field_type, columns, map_type, pot_type, field_type, field_type, total],
        [], 6, field_one, products, cell_map, pot, filter_block,
    )
    state_energy = jnp.sum(energies[:, 0, :count], axis=0) / (nodes * mesh_size)
    parts, state_energy = lax.optimization_barrier((parts, state_energy))
    states = swap(parts, "band")
    rotated_type = ((rotation_rows.shape[1], width), half)
    (rotated,) = call(
        rotate_kernel, "rotate", [rotated_type + (hbm,)], [rotated_type], [], 2,
        panel_owner, all_rows, states, places=(smem, vmem, vmem),
    )
    return (filtered, rotated, state_energy)


def solution(mesh):
    placed = (
        P("band", "mesh"),
        P("mesh"),
        P("mesh"),
        P(),
        P(None, "mesh"),
        P("mesh", None),
        P("mesh", None, None),
        P("band", None),
        P(),
    )
    return jax.shard_map(
        per_device,
        mesh=mesh,
        in_specs=placed,
        out_specs=(P("band", "mesh"), P(None, ("mesh", "band")), P("band")),
        check_vma=False,
    )
```
